32 devices in a mesh: ep: 8 (over z, x), tp: 4 (over y, core).
Axes of the slice: x: 2, y: 2, z: 4, core: 2. Of those that a mesh axis runs over, the one named last changes fastest.
Arguments:
- tokens: bfloat16 [6144, 2048], P('ep'), may hold values from -6 to 6
- lengths: int32 [8], P('ep'), may hold values from 384 to 768, as said below
- routes: int32 [6144, 4], P('ep'), may hold values from 0 to 7, all different within a row
- route_weights: float32 [6144, 4], P('ep'), may hold values from 0.1 to 0.6
- slot_order: int32 [8, 768], P('ep'), may hold values from 0 to 767, each once within a row
- norm_one_gain: bfloat16 [2048], P('ep'), may hold values from 0.5 to 1.5
- query_weight: bfloat16 [2048, 2048], P('ep', 'tp'), may hold values from -0.125 to 0.125
- key_weight: bfloat16 [2048, 2048], P('ep', 'tp'), may hold values from -0.125 to 0.125
- value_weight: bfloat16 [2048, 2048], P('ep', 'tp'), may hold values from -0.125 to 0.125
- query_bias: bfloat16 [16, 128], P('tp', 'ep'), may hold values from -3 to 3
- key_bias: bfloat16 [16, 128], P('tp', 'ep'), may hold values from -3 to 3
- value_bias: bfloat16 [16, 128], P('tp', 'ep'), may hold values from -3 to 3
- output_weight: bfloat16 [2048, 2048], P('tp', 'ep'), may hold values from -0.5 to 0.5
- norm_two_gain: bfloat16 [2048], P('ep'), may hold values from 0.5 to 1.5
- shared_gate: bfloat16 [2048, 5632], P('ep', 'tp'), may hold values from -0.125 to 0.125
- shared_up: bfloat16 [2048, 5632], P('ep', 'tp'), may hold values from -0.125 to 0.125
- shared_down: bfloat16 [5632, 2048], P('tp', 'ep'), may hold values from -0.078125 to 0.078125
- shared_switch: bfloat16 [2048], P('ep'), may hold values from -0.125 to 0.125
- expert_gate: bfloat16 [8, 2048, 1408], P('ep', None, 'tp'), may hold values from -0.125 to 0.125
- expert_up: bfloat16 [8, 2048, 1408], P('ep', None, 'tp'), may hold values from -0.125 to 0.125
- expert_down: bfloat16 [8, 1408, 2048], P('ep', 'tp'), may hold values from -0.15625 to 0.15625
- cotangent: bfloat16 [6144, 2048], P('ep'), may hold values from -6 to 6
Outputs:
- output: bfloat16 [6144, 2048], P('ep')
- grad_tokens: bfloat16 [6144, 2048], P('ep')
- grad_norm_one_gain: float32 [2048], P('ep')
- grad_query_weight: float32 [2048, 2048], P('ep', 'tp')
- grad_key_weight: float32 [2048, 2048], P('ep', 'tp')
- grad_value_weight: float32 [2048, 2048], P('ep', 'tp')
- grad_query_bias: float32 [16, 128], P('tp', 'ep')
- grad_key_bias: float32 [16, 128], P('tp', 'ep')
- grad_value_bias: float32 [16, 128], P('tp', 'ep')
- grad_output_weight: float32 [2048, 2048], P('tp', 'ep')
- grad_norm_two_gain: float32 [2048], P('ep')
- grad_shared_gate: float32 [2048, 5632], P('ep', 'tp')
- grad_shared_up: float32 [2048, 5632], P('ep', 'tp')
- grad_shared_down: float32 [5632, 2048], P('tp', 'ep')
- grad_shared_switch: float32 [2048], P('ep')
- grad_expert_gate: float32 [8, 2048, 1408], P('ep', None, 'tp')
- grad_expert_up: float32 [8, 2048, 1408], P('ep', None, 'tp')
- grad_expert_down: float32 [8, 1408, 2048], P('ep', 'tp')
The draws below stay inside these ranges and needn't reach their ends.
Inputs may be any that keep to these rules, and one draw needn't show every extreme that they name: `lengths`: each block's sequence has at least 384 tokens; some block is filled by its sequence in every draw. `routes`: each row names 4 different experts; every expert is named by some row. `slot_order`: each block's row is a permutation of 0 to 767.
All inputs are finite; a program needn't handle non-finite values.
Results may differ from the reference program's by a relative error of at most 0.028.
Values may be sent and summed in bfloat16 or wider, within the bound.
No kernel may reach another device: no remote copies, remote signals or barrier semaphores. Data moves between devices by JAX's collectives and lax.ppermute only.
A program may use at most 320 MiB of HBM per device.

```python
import math
from functools import partial
import jax
import jax.numpy as jnp
from jax import lax

D = 2048
HEADS = 16
HEAD = 128
FE = 1408
FS = 5632
TOP = 4
TOK_DEV = 768
EXPERTS = 8
TOKENS = 6144
N_EP = 8
N_TP = 4


def draw_lengths(key, part):
    draw_key, pick_key = jax.random.split(key)
    lengths_drawn = jax.random.randint(draw_key, (N_EP,), TOK_DEV // 2, TOK_DEV + 1)
    chosen = jax.random.randint(pick_key, (), 0, N_EP)
    return lengths_drawn.at[chosen].set(TOK_DEV).astype(jnp.int32)


def spiked(array, rng, source, target, shards_of, factor):
    owner, partner = [(jnp.arange(array.shape[position]) // (array.shape[position] // shards_of)).reshape([-1 if axis == position else 1 for axis in range(array.ndim)]) for position in (source, target)]
    chosen = jax.random.permutation(rng, shards_of)[partner]
    strong = (owner == chosen) | (owner == (partner + shards_of // 2) % shards_of)
    return jnp.where(strong, factor * array, array)


def level_of(own_key, extent, cuts, smallest, largest):
    factor_of, own = 1.0, jax.random.fold_in(own_key, 6)
    for position, shards_of in cuts:
        draws = jnp.exp(jax.random.uniform(jax.random.fold_in(own, position), (shards_of,), jnp.float32, smallest / len(cuts), largest / len(cuts)))
        factor_of = factor_of * jnp.repeat(draws, extent[position] // shards_of).reshape([-1 if axis == position else 1 for axis in range(len(extent))])
    return factor_of


def different_ones(own_key, rows, count, top, lift):
    sequence = jax.random.permutation(jax.random.fold_in(own_key, 1), count)
    boost = sequence
    for power in range(3):
        boost = boost * boost // count
    boost = boost * lift // count
    chance = jax.random.randint(jax.random.fold_in(own_key, 2), (rows, count), 0, 4096) + boost
    holders = jax.random.permutation(jax.random.fold_in(own_key, 3), rows)[jnp.arange(count) % rows]
    chance = jnp.where(jnp.arange(rows)[:, None] == holders[None, :], 1 << 14, chance)
    score = chance * count + jnp.arange(count)
    return lax.top_k(score.astype(jnp.int32), top)[1].astype(jnp.int32)


def scatter_about(rng, extent, spread, reach, cuts=(), held_as=jnp.bfloat16):
    drawn = jax.random.normal(rng, extent, jnp.float32) * spread
    if len(cuts) > 0:
        drawn = level_of(rng, extent, cuts, -0.22, 0.18) * drawn
    return jnp.clip(drawn, min=-reach, max=reach).astype(held_as)


def bell_draw_with(key, dims, width, most, pieces, heavy, held_as=jnp.bfloat16):
    result = width * jax.random.normal(key, dims, jnp.float32)
    if pieces:
        result = result * level_of(key, dims, pieces, -0.22, 0.18)
    return jnp.clip(spiked(result, jax.random.fold_in(key, 3), *heavy), -most, most).astype(held_as)


def setup_inputs(seed: int = 0) -> dict:
    splits = jax.random.split(jax.random.key(seed), 23)
    tokens = bell_draw_with(splits[0], (TOKENS, D), 1.0, 6.0, ((0, 8),), (0, 1, 8, 2.0))
    lengths = draw_lengths(jax.random.fold_in(splits[22], 71), 0)
    routes = different_ones(splits[2], TOKENS, EXPERTS, TOP, 4096)
    route_weights = jnp.clip(jnp.exp(math.log(0.6) - 1.7917595 * jax.random.uniform(splits[3], (TOKENS, TOP), jnp.float32) ** level_of(splits[3], (TOKENS, TOP), ((0, 8),), -0.2, 0.2)), 0.1, 0.6)
    slot_order = jax.vmap(lambda own: jax.random.permutation(own, TOK_DEV))(jax.random.split(splits[4], N_EP)).reshape((N_EP, TOK_DEV)).astype(jnp.int32)
    norm_one_gain = jnp.clip(1.0 + 0.1 * jax.random.normal(splits[5], (D,), jnp.float32), 0.5, 1.5).astype(jnp.bfloat16)
    query_weight = scatter_about(splits[6], (D, D), D ** -0.5, 0.125, ((0, 8), (1, 4)))
    key_weight = scatter_about(splits[7], (D, D), D ** -0.5, 0.125, ((0, 8), (1, 4)))
    value_weight = scatter_about(splits[8], (D, D), D ** -0.5, 0.125, ((0, 8), (1, 4)))
    query_bias = scatter_about(splits[9], (HEADS, HEAD), 0.5, 3.0, ((0, 4), (1, 8)))
    key_bias = scatter_about(splits[10], (HEADS, HEAD), 0.5, 3.0, ((0, 4), (1, 8)))
    value_bias = scatter_about(splits[11], (HEADS, HEAD), 0.5, 3.0, ((0, 4), (1, 8)))
    output_weight = scatter_about(splits[12], (D, D), (D // 16) ** -0.5, 0.5, ((0, 4), (1, 8)))
    norm_two_gain = jnp.clip(1.0 + 0.1 * jax.random.normal(splits[13], (D,), jnp.float32), 0.5, 1.5).astype(jnp.bfloat16)
    shared_gate = scatter_about(splits[14], (D, FS), D ** -0.5, 0.125, ((0, 8), (1, 4)))
    shared_up = scatter_about(splits[15], (D, FS), D ** -0.5, 0.125, ((0, 8), (1, 4)))
    shared_down = scatter_about(splits[16], (FS, D), FS ** -0.5, 0.078125, ((0, 4), (1, 8)))
    shared_switch = scatter_about(splits[17], (D,), D ** -0.5, 0.125, ((0, 8),))
    expert_gate = scatter_about(splits[18], (EXPERTS, D, FE), D ** -0.5, 0.125, ((0, 8), (2, 4)))
    expert_up = scatter_about(splits[19], (EXPERTS, D, FE), D ** -0.5, 0.125, ((0, 8), (2, 4)))
    expert_down = scatter_about(splits[20], (EXPERTS, FE, D), FE ** -0.5, 0.15625, ((0, 8), (1, 4)))
    cotangent = bell_draw_with(splits[21], (TOKENS, D), 1.0, 6.0, ((0, 8),), (0, 1, 8, 2.0))
    return dict(tokens=tokens, lengths=lengths, routes=routes, route_weights=route_weights, slot_order=slot_order, norm_one_gain=norm_one_gain, query_weight=query_weight, key_weight=key_weight, value_weight=value_weight, query_bias=query_bias, key_bias=key_bias, value_bias=value_bias, output_weight=output_weight, norm_two_gain=norm_two_gain, shared_gate=shared_gate, shared_up=shared_up, shared_down=shared_down, shared_switch=shared_switch, expert_gate=expert_gate, expert_up=expert_up, expert_down=expert_down, cotangent=cotangent)


norm_eps = 1e-06
rope_base = 1000000.0
highest = lax.Precision.HIGHEST

@jax.custom_vjp
def low(v):
    return lax.optimization_barrier(v.astype(jnp.bfloat16)).astype(jnp.float32)

@jax.custom_vjp
def low_back(v):
    return v

def low_keep(v):
    return (low(v), None)

def low_pass(kept, grad):
    return (grad,)

def back_keep(v):
    return (v, None)

def back_low(kept, grad):
    return (low(grad),)
low.defvjp(low_keep, low_pass)
low_back.defvjp(back_keep, back_low)

def rms_factor(values):
    return lax.rsqrt(lax.optimization_barrier(jnp.mean(values * values, axis=-1, keepdims=True)) + norm_eps)

def rotary_tables(row_count, head_size):
    half_size = head_size // 2
    inverse = rope_base ** (-(jnp.arange(half_size, dtype=jnp.float32) * 2.0 / head_size))
    angles = jnp.arange(row_count, dtype=jnp.float32)[:, None] * inverse[None, :]
    cosine = jnp.concatenate([jnp.cos(angles), jnp.cos(angles)], axis=1)
    sine = jnp.concatenate([jnp.sin(angles), jnp.sin(angles)], axis=1)
    return (cosine[:, None, :], sine[:, None, :])

def rotate_forward(values, cosine, sine):
    half_size = values.shape[-1] // 2
    turned = jnp.concatenate([-values[..., half_size:], values[..., :half_size]], axis=-1)
    return values * cosine + turned * sine

def slot_plan(route_rows, rank_rows, valid_rows, experts_total, capacity):
    row_count, top_count = route_rows.shape
    ordered = jnp.zeros((row_count,), jnp.int32).at[rank_rows].set(jnp.arange(row_count, dtype=jnp.int32))
    ordered_routes = route_rows[ordered]
    ordered_valid = valid_rows[ordered]
    matches = (ordered_routes[:, :, None] == jnp.arange(experts_total, dtype=jnp.int32)[None, None, :]) & ordered_valid[:, None, None]
    onehot = matches.astype(jnp.int32).reshape(row_count * top_count, experts_total)
    before = jnp.cumsum(onehot, axis=0) - onehot
    ordered_slots = lax.optimization_barrier(jnp.sum(before * onehot, axis=1)).astype(jnp.int32).reshape(row_count, top_count)
    slots = ordered_slots[rank_rows]
    kept = valid_rows[:, None] & (slots < capacity)
    target = jnp.where(kept, route_rows * capacity + slots, experts_total * capacity)
    return (kept, target.reshape(-1).astype(jnp.int32))

def attend_block(operands):
    queries, keys, values, length_now = operands
    scores = jnp.einsum('thd,shd->hts', queries, keys, precision=highest) * HEAD ** (-0.5)
    scores = low_back(scores)
    rows_at = jnp.arange(TOK_DEV, dtype=jnp.int32)[:, None]
    cols_at = jnp.arange(TOK_DEV, dtype=jnp.int32)[None, :]
    allowed = (cols_at <= rows_at) & (cols_at < length_now)
    scores = jnp.where(allowed[None], scores, -1e+30)
    peak = lax.optimization_barrier(jnp.max(scores, axis=-1, keepdims=True))
    raised = jnp.exp(scores - peak)
    probs = raised / lax.optimization_barrier(jnp.sum(raised, axis=-1, keepdims=True))
    return jnp.einsum('hts,shd->thd', low(probs), values, precision=highest)

def reference(tokens, lengths, routes, route_weights, slot_order, norm_one_gain, query_weight, key_weight, value_weight, query_bias, key_bias, value_bias, output_weight, norm_two_gain, shared_gate, shared_up, shared_down, shared_switch, expert_gate, expert_up, expert_down, cotangent):
    capacity = TOK_DEV * TOP // EXPERTS
    slot_total = EXPERTS * capacity
    valid_rows = jnp.arange(TOK_DEV, dtype=jnp.int32)[None, :] < lengths[:, None]
    valid_float = valid_rows.reshape(TOKENS).astype(jnp.float32)[:, None]
    kept, target = jax.vmap(partial(slot_plan, experts_total=EXPERTS, capacity=capacity))(routes.reshape(N_EP, TOK_DEV, TOP), slot_order, valid_rows)
    pair_token = jnp.repeat(jnp.arange(TOK_DEV, dtype=jnp.int32), TOP)
    sources = jnp.arange(N_EP, dtype=jnp.int32)[:, None] * TOK_DEV + pair_token[None, :]
    pair_weight = jnp.where(kept, route_weights.reshape(N_EP, TOK_DEV, TOP), 0.0).reshape(N_EP, -1).astype(jnp.float32)

    def fill_table(target_row, source_row, weight_row):
        table = jnp.full((slot_total + 1,), TOKENS, jnp.int32).at[target_row].set(source_row)
        scale_row = jnp.zeros((slot_total + 1,), jnp.float32).at[target_row].set(weight_row)
        return (table[:slot_total], scale_row[:slot_total])
    tables, scales = jax.vmap(fill_table)(target, sources, pair_weight)
    tables = tables.reshape(N_EP, EXPERTS, capacity).transpose(1, 0, 2).reshape(EXPERTS, -1)
    scales = scales.reshape(N_EP, EXPERTS, capacity).transpose(1, 0, 2).reshape(EXPERTS, -1)
    cosine, sine = rotary_tables(TOK_DEV, HEAD)
    part_width = FE // N_TP

    def forward(inputs, params):
        gain_one, query_mat, key_mat, value_mat, query_add, key_add, value_add, output_mat, gain_two, shared_gate_mat, shared_up_mat, shared_down_mat, switch_vector, expert_gate_mat, expert_up_mat, expert_down_mat = params
        normed_one = low(inputs * rms_factor(inputs) * gain_one)

        def project(matrix, offset):
            return low_back(jnp.dot(normed_one, matrix, precision=highest) + offset.reshape(-1))
        query_pre = project(query_mat, query_add).reshape(N_EP, TOK_DEV, HEADS, HEAD)
        key_pre = project(key_mat, key_add).reshape(N_EP, TOK_DEV, HEADS, HEAD)
        queries = low(rotate_forward(query_pre, cosine, sine))
        keys = low(rotate_forward(key_pre, cosine, sine))
        values = low(project(value_mat, value_add).reshape(N_EP, TOK_DEV, HEADS, HEAD))
        attended = lax.map(jax.checkpoint(attend_block), (queries, keys, values, lengths))
        attended = low(low_back(attended.reshape(TOKENS, D)))
        hidden = inputs + low_back(jnp.dot(attended, output_mat, precision=highest))
        normed_two = low(hidden * rms_factor(hidden) * gain_two)
        padded_rows = jnp.concatenate([normed_two, jnp.zeros((1, D), jnp.float32)], axis=0)

        def expert_step(running, operands):
            table, scale_row, gate_mat, up_mat, down_mat = operands
            rows = padded_rows[table]
            produced = jnp.zeros((table.shape[0], D), jnp.float32)
            for group_index in range(N_TP):
                lower = group_index * part_width
                entered = low_back(rows)
                gate_act = low_back(jnp.dot(entered, gate_mat[:, lower:lower + part_width], precision=highest))
                up_act = low_back(jnp.dot(entered, up_mat[:, lower:lower + part_width], precision=highest))
                inner = low(jax.nn.silu(gate_act) * up_act)
                produced = produced + low(jnp.dot(inner, down_mat[lower:lower + part_width, :], precision=highest))
            produced = low_back(produced)
            running = running.at[table].add(produced * scale_row[:, None], mode='drop')
            return (running, None)
        expert_mix, unused = lax.scan(jax.checkpoint(expert_step), jnp.zeros((TOKENS, D), jnp.float32), (tables, scales, expert_gate_mat, expert_up_mat, expert_down_mat))
        shared_gate_act = low_back(jnp.dot(normed_two, shared_gate_mat, precision=highest))
        shared_up_act = low_back(jnp.dot(normed_two, shared_up_mat, precision=highest))
        shared_inner = low(jax.nn.silu(shared_gate_act) * shared_up_act)
        shared_out = low_back(jnp.dot(shared_inner, shared_down_mat, precision=highest))
        switch_value = jax.nn.sigmoid(jnp.dot(normed_two, switch_vector, precision=highest))
        return valid_float * (hidden + expert_mix + switch_value[:, None] * shared_out)
    params = tuple((weight_item.astype(jnp.float32) for weight_item in (norm_one_gain, query_weight, key_weight, value_weight, query_bias, key_bias, value_bias, output_weight, norm_two_gain, shared_gate, shared_up, shared_down, shared_switch, expert_gate, expert_up, expert_down)))
    output, pullback = jax.vjp(forward, tokens.astype(jnp.float32), params)
    token_gradient, parameter_gradients = pullback(cotangent.astype(jnp.float32))
    first_gain_gradient, query_gradient, key_gradient, value_gradient, query_offset_gradient, key_offset_gradient, value_offset_gradient, output_gradient, second_gain_gradient, shared_gate_gradient, shared_up_gradient, shared_down_gradient, switch_gradient, expert_gate_gradient, expert_up_gradient, expert_down_gradient = parameter_gradients
    return (output.astype(jnp.bfloat16), token_gradient.astype(jnp.bfloat16), first_gain_gradient, query_gradient, key_gradient, value_gradient, query_offset_gradient, key_offset_gradient, value_offset_gradient, output_gradient, second_gain_gradient, shared_gate_gradient, shared_up_gradient, shared_down_gradient, switch_gradient, expert_gate_gradient, expert_up_gradient, expert_down_gradient)
```

```python
import jax
import jax.numpy as jnp
from jax import lax
from jax.sharding import PartitionSpec as P

norm_eps = 1e-06
rope_base = 1000000.0


def rms_factor(values):
    return lax.rsqrt(jnp.mean(values * values, axis=-1, keepdims=True) + norm_eps)


def rotary_tables(row_count, head_size):
    half_size = head_size // 2
    inverse = rope_base ** (-(jnp.arange(half_size, dtype=jnp.float32) * 2.0 / head_size))
    angles = jnp.arange(row_count, dtype=jnp.float32)[:, None] * inverse[None, :]
    cosine = jnp.concatenate([jnp.cos(angles), jnp.cos(angles)], axis=1)
    sine = jnp.concatenate([jnp.sin(angles), jnp.sin(angles)], axis=1)
    return (cosine[:, None, :], sine[:, None, :])


def rotate_forward(values, cosine, sine):
    half_size = values.shape[-1] // 2
    turned = jnp.concatenate([-values[..., half_size:], values[..., :half_size]], axis=-1)
    return values * cosine + turned * sine


def rotate_backward(grads, cosine, sine):
    half_size = grads.shape[-1] // 2
    scaled = grads * sine
    turned = jnp.concatenate([scaled[..., half_size:], -scaled[..., :half_size]], axis=-1)
    return grads * cosine + turned


def times(left, right):
    return jnp.dot(left, right, preferred_element_type=jnp.float32)


def contract_rows(left, right):
    return lax.dot_general(
        left, right, (((0,), (0,)), ((), ())), preferred_element_type=jnp.float32
    )


def times_transpose(left, right):
    return lax.dot_general(
        left, right, (((1,), (1,)), ((), ())), preferred_element_type=jnp.float32
    )


def low(values):
    return values.astype(jnp.bfloat16)


def masked_scores(queries, keys, length_now, score_scale):
    scores = (
        jnp.einsum("thd,shd->hts", queries, keys, preferred_element_type=jnp.float32) * score_scale
    )
    row_count = queries.shape[0]
    rows_at = jnp.arange(row_count)[:, None]
    cols_at = jnp.arange(row_count)[None, :]
    allowed = (cols_at <= rows_at) & (cols_at < length_now)
    return jnp.where(allowed[None], scores, -1e30)


def slot_plan(route_rows, rank_rows, valid_rows, experts_total, capacity):
    row_count, top_count = route_rows.shape
    ordered = (
        jnp.zeros((row_count,), jnp.int32).at[rank_rows].set(jnp.arange(row_count, dtype=jnp.int32))
    )
    ordered_routes = route_rows[ordered]
    ordered_valid = valid_rows[ordered]
    matches = (
        ordered_routes[:, :, None] == jnp.arange(experts_total, dtype=jnp.int32)[None, None, :]
    ) & ordered_valid[:, None, None]
    onehot = matches.astype(jnp.int32).reshape(row_count * top_count, experts_total)
    before = jnp.cumsum(onehot, axis=0) - onehot
    ordered_slots = jnp.sum(before * onehot, axis=1).reshape(row_count, top_count)
    slots = ordered_slots[rank_rows]
    kept = valid_rows[:, None] & (slots < capacity)
    return (kept, slots)


def ring_order(count):
    return [*range(0, count, 2), *range(count - 1, 0, -2)]


def ring_pairs(count, step):
    order = ring_order(count)
    return [(order[i], order[(i + step) % count]) for i in range(count)]


def ring_place(count):
    order = ring_order(count)
    places = [order.index(i) for i in range(count)]
    return jnp.array(places, jnp.int32)[lax.axis_index("ep")]


def ring_member(count, place):
    order = jnp.array(ring_order(count), jnp.int32)
    return order[lax.rem(place + count, count)]


def forth(values, count):
    return lax.ppermute(values, "ep", ring_pairs(count, 1))


def back(values, count):
    return lax.ppermute(values, "ep", ring_pairs(count, -1))


def ring_gather(shard, axis):
    count = lax.axis_size("ep")
    place = ring_place(count)
    half = count // 2
    size = shard.shape[axis]
    shape = list(shard.shape)
    shape[axis] = size * count
    cut = shard.shape[0] // 2

    def put(full, piece, owner, offset=0):
        at = [0, 0]
        at[axis] = owner * size
        at[0] = at[0] + offset
        return lax.dynamic_update_slice(full, piece, tuple(jnp.asarray(i, jnp.int32) for i in at))

    full = put(jnp.zeros(shape, shard.dtype), shard, lax.axis_index("ep"))
    ahead, behind = shard, shard
    for step in range(1, half):
        ahead, behind = forth(ahead, count), back(behind, count)
        full = put(full, ahead, ring_member(count, place - step))
        full = put(full, behind, ring_member(count, place + step))
    top, bottom = forth(ahead[:cut], count), back(behind[cut:], count)
    far = ring_member(count, place + half)
    full = put(full, top, far)
    return put(full, bottom, far, cut)


def ring_scatter(full, axis):
    count = lax.axis_size("ep")
    place = ring_place(count)
    half = count // 2
    size = full.shape[axis] // count

    def take(step):
        return lax.dynamic_slice_in_dim(
            full, ring_member(count, place + step) * size, size, axis
        ).astype(jnp.float32)

    far = take(half)
    cut = far.shape[0] // 2
    ahead, behind = forth(low(far[:cut]), count), back(low(far[cut:]), count)
    for step in range(half - 1, 0, -1):
        after, before = take(step), take(-step)
        if step == half - 1:
            after = jnp.concatenate([after[:cut] + ahead.astype(jnp.float32), after[cut:]], axis=0)
            before = jnp.concatenate(
                [before[:cut], before[cut:] + behind.astype(jnp.float32)], axis=0
            )
        else:
            after = after + ahead.astype(jnp.float32)
            before = before + behind.astype(jnp.float32)
        ahead, behind = forth(low(after), count), back(low(before), count)
    return take(0) + ahead.astype(jnp.float32) + behind.astype(jnp.float32)


def inner(values):
    return lax.ppermute(values, "tp", [(i, i ^ 1) for i in range(4)])


def outer(values):
    return lax.ppermute(values, "tp", [(i, i ^ 2) for i in range(4)])


def tp_place():
    member = lax.axis_index("tp")
    return lax.div(member, 2), lax.rem(member, 2)


def rows_scatter(partial):
    outer_at, inner_at = tp_place()
    rows, width = partial.shape
    split = partial.reshape(2, 2, rows // 4, width)
    arrived = inner(lax.dynamic_index_in_dim(split, 1 - inner_at, 1, keepdims=False))
    mine = lax.dynamic_index_in_dim(split, inner_at, 1, keepdims=False)
    summed = mine.astype(jnp.float32) + arrived.astype(jnp.float32)
    sent = low(lax.dynamic_index_in_dim(summed, 1 - outer_at, 0, keepdims=False))
    kept = lax.dynamic_index_in_dim(summed, outer_at, 0, keepdims=False)
    return kept + outer(sent).astype(jnp.float32)


def rows_gather(rows):
    outer_at, inner_at = tp_place()
    count, width = rows.shape
    beside = inner(rows)
    across = outer(rows)
    diagonal = inner(across)
    full = jnp.zeros((4 * count, width), rows.dtype)

    def put(full, piece, outer_now, inner_now):
        at = (outer_now * 2 + inner_now) * count
        return lax.dynamic_update_slice(full, piece, (at, jnp.zeros_like(at)))

    full = put(full, rows, outer_at, inner_at)
    full = put(full, beside, outer_at, 1 - inner_at)
    full = put(full, across, 1 - outer_at, inner_at)
    return put(full, diagonal, 1 - outer_at, 1 - inner_at)


def tp_pieces(own):
    beside, across = inner(own), outer(own)
    return [own, beside, across, inner(across)]


def tp_reduce(pieces):
    own, beside, across, diagonal = pieces
    own = own.astype(jnp.float32) + inner(beside).astype(jnp.float32)
    across = across.astype(jnp.float32) + inner(diagonal).astype(jnp.float32)
    return own + outer(low(across)).astype(jnp.float32)


def tp_sum(values):
    values = values + inner(values)
    return values + outer(values)


def exchange(rows):
    return lax.all_to_all(rows, "ep", split_axis=0, concat_axis=0, tiled=True)


def body(
    tokens,
    lengths,
    routes,
    route_weights,
    slot_order,
    norm_one_gain,
    query_weight,
    key_weight,
    value_weight,
    query_bias,
    key_bias,
    value_bias,
    output_weight,
    norm_two_gain,
    shared_gate,
    shared_up,
    shared_down,
    shared_switch,
    expert_gate,
    expert_up,
    expert_down,
    cotangent,
):
    ep_count = lax.axis_size("ep")
    row_count, model_width = tokens.shape
    heads_here, bias_part = query_bias.shape
    head_size = bias_part * ep_count
    heads_width = heads_here * head_size
    shared_hidden = shared_gate.shape[1]
    expert_hidden = expert_gate.shape[2]
    gain_part = norm_one_gain.shape[0]
    tp_at = lax.axis_index("tp")
    own_count = row_count // 4
    own_start = tp_at * own_count

    def own_rows(values):
        return lax.dynamic_slice_in_dim(values, own_start, own_count, 0)

    full_qkv = ring_gather(jnp.concatenate([query_weight, key_weight, value_weight], axis=1), 0)
    full_output = ring_gather(output_weight, 1)
    small = jnp.concatenate(
        [
            norm_one_gain,
            norm_two_gain,
            shared_switch,
            query_bias.reshape(-1),
            key_bias.reshape(-1),
            value_bias.reshape(-1),
        ]
    )
    small = lax.all_gather(small, "ep", axis=0, tiled=False)
    gain_one = small[:, :gain_part].reshape(-1).astype(jnp.float32)
    gain_two = small[:, gain_part : 2 * gain_part].reshape(-1).astype(jnp.float32)
    full_switch = small[:, 2 * gain_part : 3 * gain_part].reshape(-1)
    bias_all = (
        small[:, 3 * gain_part :]
        .reshape(ep_count, 3 * heads_here, bias_part)
        .transpose(1, 0, 2)
        .reshape(-1)
        .astype(jnp.float32)
    )
    full_shared = ring_gather(jnp.concatenate([shared_gate, shared_up], axis=1), 0)
    full_down = ring_gather(shared_down, 1)

    group = -(-expert_hidden // 128) * 128
    spare = group - expert_hidden
    gates = [jnp.pad(g, ((0, 0), (0, spare))) for g in tp_pieces(expert_gate[0])]
    ups = [jnp.pad(u, ((0, 0), (0, spare))) for u in tp_pieces(expert_up[0])]
    downs = [jnp.pad(d, ((0, spare), (0, 0))) for d in tp_pieces(expert_down[0])]
    expert_in = jnp.concatenate(gates + ups, axis=1)
    expert_out = jnp.concatenate(downs, axis=0)
    expert_width = 4 * group

    score_scale = head_size ** (-0.5)
    length_now = lengths[0]
    valid_rows = jnp.arange(row_count) < length_now
    valid_float = valid_rows.astype(jnp.float32)[:, None]
    experts_total = ep_count
    top_count = routes.shape[1]
    capacity = row_count * top_count // experts_total
    slots_here = capacity // 4
    slot_rows = experts_total * slots_here
    kept, slots = slot_plan(routes, slot_order[0], valid_rows, experts_total, capacity)
    slots = slots - tp_at * slots_here
    taken = kept & (slots >= 0) & (slots < slots_here)
    target = jnp.where(taken, routes * slots_here + slots, -1)
    slot_ids = jnp.arange(slot_rows, dtype=jnp.int32)[:, None]
    select = jnp.zeros((slot_rows, row_count), jnp.float32)
    weighted = jnp.zeros((slot_rows, row_count), jnp.float32)
    for choice in range(top_count):
        hit = slot_ids == target[:, choice][None, :]
        select = jnp.where(hit, 1.0, select)
        weighted = jnp.where(hit, route_weights[:, choice][None, :], weighted)
    select, weighted = low(select), low(weighted)

    grad_low = jnp.where(valid_rows[:, None], cotangent, jnp.zeros_like(cotangent))
    grad_out = grad_low.astype(jnp.float32)
    grad_sent = low(times(weighted, grad_low)).reshape(experts_total, slots_here, model_width)
    grad_arrived = exchange(grad_sent).reshape(slot_rows, model_width)

    inputs = tokens.astype(jnp.float32)
    factor_one = rms_factor(inputs)
    normed_one = low(inputs * factor_one * gain_one)
    cosine, sine = rotary_tables(row_count, head_size)
    qkv = times(normed_one, full_qkv) + bias_all
    query_pre, key_pre, value_pre = (
        qkv[:, i * heads_width : (i + 1) * heads_width].reshape(row_count, heads_here, head_size)
        for i in range(3)
    )
    queries = low(rotate_forward(query_pre, cosine, sine))
    keys_rot = low(rotate_forward(key_pre, cosine, sine))
    values = low(value_pre)
    scores = masked_scores(queries, keys_rot, length_now, score_scale)
    peak = jnp.max(scores, axis=-1, keepdims=True)
    raised = jnp.exp(scores - peak)
    totals = jnp.sum(raised, axis=-1, keepdims=True)
    probs = raised / totals
    log_total = peak + jnp.log(totals)
    attended = jnp.einsum("hts,shd->thd", low(probs), values, preferred_element_type=jnp.float32)
    attended_low = low(attended.reshape(row_count, -1))
    own_inputs = own_rows(tokens).astype(jnp.float32)
    hidden = own_inputs + rows_scatter(low(times(attended_low, full_output)))
    factor_two = rms_factor(hidden)
    own_normed_two = low(hidden * factor_two * gain_two)
    normed_two = rows_gather(own_normed_two)

    sent = low(times(select, normed_two)).reshape(experts_total, slots_here, model_width)
    arrived = exchange(sent).reshape(slot_rows, model_width)
    act = times(arrived, expert_in)
    gate_act, up_act = act[:, :expert_width], act[:, expert_width:]
    sigma = jax.nn.sigmoid(gate_act)
    swish = gate_act * sigma
    inner_act = low(swish * up_act)
    inner_grad = times_transpose(grad_arrived, expert_out)
    up_grad = low(inner_grad * swish)
    gate_grad = low(inner_grad * up_act * sigma * (1.0 + gate_act * (1.0 - sigma)))
    both_grad = jnp.concatenate([gate_grad, up_grad], axis=1)
    back_rows = low(times_transpose(both_grad, expert_in))
    back_home = exchange(back_rows.reshape(experts_total, slots_here, model_width))
    back_home = back_home.reshape(slot_rows, model_width)
    produced = low(times(inner_act, expert_out))
    produced_home = exchange(produced.reshape(experts_total, slots_here, model_width))
    produced_home = produced_home.reshape(slot_rows, model_width)
    grad_in = low(contract_rows(arrived, both_grad))
    grad_down = low(contract_rows(inner_act, grad_arrived))

    def columns(start):
        return [
            grad_in[:, start + i * group : start + i * group + expert_hidden] for i in range(4)
        ]

    grad_expert_gate = tp_reduce(columns(0))[None]
    grad_expert_up = tp_reduce(columns(expert_width))[None]
    grad_expert_down = tp_reduce(
        [grad_down[i * group : i * group + expert_hidden] for i in range(4)]
    )[None]

    shared_act = times(normed_two, full_shared)
    shared_gate_act, shared_up_act = shared_act[:, :shared_hidden], shared_act[:, shared_hidden:]
    shared_sigma = jax.nn.sigmoid(shared_gate_act)
    shared_swish = shared_gate_act * shared_sigma
    shared_inner = low(shared_swish * shared_up_act)
    shared_part = times(shared_inner, full_down)
    switch_value = jax.nn.sigmoid(
        jnp.sum(normed_two.astype(jnp.float32) * full_switch.astype(jnp.float32), axis=1)
    )
    shared_out_grad = low(switch_value[:, None] * grad_out)
    shared_inner_grad = times_transpose(shared_out_grad, full_down)
    shared_up_grad = low(shared_inner_grad * shared_swish)
    shared_gate_grad = low(
        shared_inner_grad
        * shared_up_act
        * shared_sigma
        * (1.0 + shared_gate_act * (1.0 - shared_sigma))
    )
    shared_grad = jnp.concatenate([shared_gate_grad, shared_up_grad], axis=1)
    switch_total = tp_sum(jnp.sum(grad_out * shared_part, axis=1).reshape(-1, 128)).reshape(-1)
    logit_grad = switch_total * switch_value * (1.0 - switch_value)
    normed_two_part = times_transpose(shared_grad, full_shared) + contract_rows(select, back_home)
    normed_two_grad = rows_scatter(low(normed_two_part))
    grad_shared = ring_scatter(low(contract_rows(normed_two, shared_grad)), 0)
    grad_shared_gate, grad_shared_up = grad_shared[:, :shared_hidden], grad_shared[:, shared_hidden:]
    grad_shared_down = ring_scatter(low(contract_rows(shared_inner, shared_out_grad)), 1)

    mixed = contract_rows(weighted, produced_home) + switch_value[:, None] * shared_part
    own_valid = own_rows(valid_float)
    output = rows_gather(low(own_valid * (hidden + rows_scatter(low(mixed)))))

    own_logit_grad = own_rows(logit_grad)[:, None]
    normed_two_grad = normed_two_grad + own_logit_grad * full_switch.astype(jnp.float32)[None, :]
    switch_gradient = jnp.sum(own_logit_grad * own_normed_two.astype(jnp.float32), axis=0)
    second_gain_gradient = jnp.sum(normed_two_grad * hidden * factor_two, axis=0)
    scaled_two = normed_two_grad * gain_two
    hidden_grad = (
        own_rows(grad_out)
        + factor_two * scaled_two
        - hidden * factor_two**3 * jnp.mean(scaled_two * hidden, axis=-1, keepdims=True)
    )
    attn_grad_low = rows_gather(low(hidden_grad))

    grad_output_weight = ring_scatter(low(contract_rows(attended_low, attn_grad_low)), 1)
    attended_grad = low(
        times_transpose(attn_grad_low, full_output).reshape(row_count, heads_here, head_size)
    )
    scores_again = masked_scores(queries, keys_rot, length_now, score_scale)
    probs_again = jnp.exp(scores_again - log_total)
    value_grad = jnp.einsum(
        "hts,thd->shd", low(probs_again), attended_grad, preferred_element_type=jnp.float32
    )
    probs_grad = jnp.einsum(
        "thd,shd->hts", attended_grad, values, preferred_element_type=jnp.float32
    )
    row_dot = jnp.sum(probs_again * probs_grad, axis=-1, keepdims=True)
    score_grad = low(probs_again * (probs_grad - row_dot))
    query_grad = (
        jnp.einsum("hts,shd->thd", score_grad, keys_rot, preferred_element_type=jnp.float32)
        * score_scale
    )
    key_grad = (
        jnp.einsum("hts,thd->shd", score_grad, queries, preferred_element_type=jnp.float32)
        * score_scale
    )
    query_pre_grad = low(rotate_backward(query_grad, cosine, sine).reshape(row_count, -1))
    key_pre_grad = low(rotate_backward(key_grad, cosine, sine).reshape(row_count, -1))
    value_pre_grad = low(value_grad.reshape(row_count, -1))
    qkv_grad = jnp.concatenate([query_pre_grad, key_pre_grad, value_pre_grad], axis=1)
    bias_grad = jnp.sum(qkv_grad.astype(jnp.float32), axis=0)
    normed_one_grad = rows_scatter(low(times_transpose(qkv_grad, full_qkv)))
    grad_qkv = ring_scatter(low(contract_rows(normed_one, qkv_grad)), 0)
    grad_query_weight, grad_key_weight, grad_value_weight = (
        grad_qkv[:, i * heads_width : (i + 1) * heads_width] for i in range(3)
    )
    own_factor = own_rows(factor_one)
    first_gain_gradient = jnp.sum(normed_one_grad * own_inputs * own_factor, axis=0)
    scaled_one = normed_one_grad * gain_one
    token_gradient = (
        hidden_grad
        + own_factor * scaled_one
        - own_inputs * own_factor**3 * jnp.mean(scaled_one * own_inputs, axis=-1, keepdims=True)
    )
    token_gradient = rows_gather(low(token_gradient))

    row_sums = tp_sum(jnp.stack([first_gain_gradient, second_gain_gradient, switch_gradient]))
    small_grad = jnp.concatenate(
        [
            row_sums.reshape(3, ep_count, gain_part).transpose(1, 0, 2).reshape(ep_count, -1),
            bias_grad.reshape(3 * heads_here, ep_count, bias_part)
            .transpose(1, 0, 2)
            .reshape(ep_count, -1),
        ],
        axis=1,
    )
    small_grad = lax.psum_scatter(small_grad, "ep", scatter_dimension=0, tiled=True)[0]
    first_gain_gradient, second_gain_gradient, switch_gradient = (
        small_grad[i * gain_part : (i + 1) * gain_part] for i in range(3)
    )
    bias_size = heads_here * bias_part
    grad_query_bias, grad_key_bias, grad_value_bias = (
        small_grad[3 * gain_part + i * bias_size : 3 * gain_part + (i + 1) * bias_size].reshape(
            heads_here, bias_part
        )
        for i in range(3)
    )
    return (
        output,
        token_gradient,
        first_gain_gradient,
        grad_query_weight,
        grad_key_weight,
        grad_value_weight,
        grad_query_bias,
        grad_key_bias,
        grad_value_bias,
        grad_output_weight,
        second_gain_gradient,
        grad_shared_gate,
        grad_shared_up,
        grad_shared_down,
        switch_gradient,
        grad_expert_gate,
        grad_expert_up,
        grad_expert_down,
    )


def solution(mesh):
    in_specs = (
        P("ep", None),
        P("ep"),
        P("ep", None),
        P("ep", None),
        P("ep", None),
        P("ep"),
        P("ep", "tp"),
        P("ep", "tp"),
        P("ep", "tp"),
        P("tp", "ep"),
        P("tp", "ep"),
        P("tp", "ep"),
        P("tp", "ep"),
        P("ep"),
        P("ep", "tp"),
        P("ep", "tp"),
        P("tp", "ep"),
        P("ep"),
        P("ep", None, "tp"),
        P("ep", None, "tp"),
        P("ep", "tp", None),
        P("ep", None),
    )
    out_specs = (
        P("ep", None),
        P("ep", None),
        P("ep"),
        P("ep", "tp"),
        P("ep", "tp"),
        P("ep", "tp"),
        P("tp", "ep"),
        P("tp", "ep"),
        P("tp", "ep"),
        P("tp", "ep"),
        P("ep"),
        P("ep", "tp"),
        P("ep", "tp"),
        P("tp", "ep"),
        P("ep"),
        P("ep", None, "tp"),
        P("ep", None, "tp"),
        P("ep", "tp", None),
    )
    return jax.shard_map(body, mesh=mesh, in_specs=in_specs, out_specs=out_specs, check_vma=False)
```

```python
import jax
import jax.numpy as jnp
from jax import lax
from jax.sharding import PartitionSpec as P


norm_eps = 1e-06
rope_base = 1000000.0


def rms_factor(values):
    return lax.rsqrt(jnp.mean(values * values, axis=-1, keepdims=True) + norm_eps)


def rotary_tables(row_count, head_size):
    half_size = head_size // 2
    inverse = rope_base ** (-(jnp.arange(half_size, dtype=jnp.float32) * 2.0 / head_size))
    angles = jnp.arange(row_count, dtype=jnp.float32)[:, None] * inverse[None, :]
    cosine = jnp.concatenate([jnp.cos(angles), jnp.cos(angles)], axis=1)
    sine = jnp.concatenate([jnp.sin(angles), jnp.sin(angles)], axis=1)
    return (cosine[None], sine[None])


def rotate_forward(values, cosine, sine):
    half_size = values.shape[-1] // 2
    turned = jnp.concatenate([-values[..., half_size:], values[..., :half_size]], axis=-1)
    return values * cosine + turned * sine


def rotate_backward(grads, cosine, sine):
    half_size = grads.shape[-1] // 2
    scaled = grads * sine
    turned = jnp.concatenate([scaled[..., half_size:], -scaled[..., :half_size]], axis=-1)
    return grads * cosine + turned


def by_head(values, heads):
    size = values.shape[1] // heads
    return jnp.stack([values[:, h * size : (h + 1) * size] for h in range(heads)])


def side_by_side(values):
    return jnp.concatenate([values[h] for h in range(values.shape[0])], axis=1)


def times(left, right):
    return jnp.dot(left, right, preferred_element_type=jnp.float32)


def contract_rows(left, right):
    return lax.dot_general(
        left, right, (((0,), (0,)), ((), ())), preferred_element_type=jnp.float32
    )


def times_transpose(left, right):
    return lax.dot_general(
        left, right, (((1,), (1,)), ((), ())), preferred_element_type=jnp.float32
    )


def low(values):
    return values.astype(jnp.bfloat16)


def masked_scores(queries, keys, length_now, score_scale):
    scores = (
        jnp.einsum("htd,hsd->hts", queries, keys, preferred_element_type=jnp.float32) * score_scale
    )
    row_count = queries.shape[1]
    rows_at = jnp.arange(row_count)[:, None]
    cols_at = jnp.arange(row_count)[None, :]
    allowed = (cols_at <= rows_at) & (cols_at < length_now)
    return jnp.where(allowed[None], scores, -1e30)


def slot_plan(route_rows, rank_rows, valid_rows, experts_total, capacity):
    experts = jnp.arange(experts_total, dtype=jnp.int32)
    chosen = jnp.any(route_rows[:, :, None] == experts[None, None, :], axis=1)
    chosen = low(chosen & valid_rows[:, None])
    earlier = low(rank_rows[None, :] < rank_rows[:, None])
    counts = times(earlier, chosen).astype(jnp.int32)
    mine = route_rows[:, :, None] == experts[None, None, :]
    slots = jnp.sum(jnp.where(mine, counts[:, None, :], 0), axis=2)
    kept = valid_rows[:, None] & (slots < capacity)
    return (kept, slots)


def ring_order(count):
    return [*range(0, count, 2), *range(count - 1, 0, -2)]


def take_blocks(values, order, axis):
    size = values.shape[axis] // len(order)
    return jnp.concatenate(
        [lax.slice_in_dim(values, i * size, (i + 1) * size, axis=axis) for i in order], axis=axis
    )


def to_ring(values, axis):
    return take_blocks(values, ring_order(lax.axis_size("ep")), axis)


def from_ring(values, axis):
    order = ring_order(lax.axis_size("ep"))
    return take_blocks(values, [order.index(i) for i in range(len(order))], axis)


def ring_gather(shard):
    return lax.all_gather(
        shard, "ep", axis=0, tiled=True, axis_index_groups=[ring_order(lax.axis_size("ep"))]
    )


def ring_scatter(full):
    return lax.psum_scatter(
        full,
        "ep",
        scatter_dimension=0,
        tiled=True,
        axis_index_groups=[ring_order(lax.axis_size("ep"))],
    )


def after(values, *tokens):
    return lax.optimization_barrier((values, *tokens))[0]


def pair_up(values, distance):
    count = lax.axis_size("ep")
    return lax.ppermute(values, "ep", [(i, i ^ distance) for i in range(count)])


def small_gather(row):
    count = lax.axis_size("ep")
    index = lax.axis_index("ep")
    zero = jnp.zeros_like(index)
    full = jnp.broadcast_to(row[None], (count, row.shape[0]))
    distance = 1
    while distance < count:
        start = lax.div(index, distance) * distance
        other = start + distance - 2 * lax.rem(start, 2 * distance)
        block = lax.dynamic_slice(full, (start, zero), (distance, row.shape[0]))
        full = lax.dynamic_update_slice(full, pair_up(block, distance), (other, zero))
        distance *= 2
    return full


def small_scatter(rows):
    index = lax.axis_index("ep")
    distance = lax.axis_size("ep") // 2
    while distance >= 1:
        mine = lax.rem(lax.div(index, distance), 2)
        halves = rows.reshape(2, distance, rows.shape[1])
        kept = lax.dynamic_index_in_dim(halves, mine, 0, keepdims=False)
        sent = lax.dynamic_index_in_dim(halves, 1 - mine, 0, keepdims=False)
        rows = kept + pair_up(sent, distance)
        distance //= 2
    return rows[0]


def inner(values):
    return lax.ppermute(values, "tp", [(i, i ^ 1) for i in range(4)])


def outer(values):
    return lax.ppermute(values, "tp", [(i, i ^ 2) for i in range(4)])


def tp_place():
    member = lax.axis_index("tp")
    return lax.div(member, 2), lax.rem(member, 2)


def rows_scatter(partial):
    outer_at, inner_at = tp_place()
    rows, width = partial.shape
    split = partial.reshape(2, 2, rows // 4, width)
    arrived = inner(lax.dynamic_index_in_dim(split, 1 - inner_at, 1, keepdims=False))
    mine = lax.dynamic_index_in_dim(split, inner_at, 1, keepdims=False)
    summed = mine.astype(jnp.float32) + arrived.astype(jnp.float32)
    sent = low(lax.dynamic_index_in_dim(summed, 1 - outer_at, 0, keepdims=False))
    kept = lax.dynamic_index_in_dim(summed, outer_at, 0, keepdims=False)
    arrived = outer(sent)
    return kept + arrived.astype(jnp.float32), sent


def rows_gather(rows):
    outer_at, inner_at = tp_place()
    count, width = rows.shape
    across = outer(rows)
    beside = inner(rows)
    diagonal = inner(across)
    full = jnp.zeros((4 * count, width), rows.dtype)

    def put(full, piece, outer_now, inner_now):
        at = (outer_now * 2 + inner_now) * count
        return lax.dynamic_update_slice(full, piece, (at, jnp.zeros_like(at)))

    full = put(full, rows, outer_at, inner_at)
    full = put(full, beside, outer_at, 1 - inner_at)
    full = put(full, across, 1 - outer_at, inner_at)
    return put(full, diagonal, 1 - outer_at, 1 - inner_at)


def tp_pieces(own):
    across = outer(own)
    beside = inner(own)
    return [own, beside, across, inner(across)]


def tp_reduce(pieces):
    own, beside, across, diagonal = pieces
    near = inner(beside)
    sent = low(across.astype(jnp.float32) + inner(diagonal).astype(jnp.float32))
    far = outer(sent)
    return (own, near, far), sent


def add_terms(terms):
    own, near, far = (term.astype(jnp.float32) for term in terms)
    return own + near + far


def tp_sum(values):
    values = values + inner(values)
    return values + outer(values)


def exchange(rows):
    return lax.all_to_all(rows, "ep", split_axis=0, concat_axis=0, tiled=True)


def body(
    tokens,
    lengths,
    routes,
    route_weights,
    slot_order,
    norm_one_gain,
    query_weight,
    key_weight,
    value_weight,
    query_bias,
    key_bias,
    value_bias,
    output_weight,
    norm_two_gain,
    shared_gate,
    shared_up,
    shared_down,
    shared_switch,
    expert_gate,
    expert_up,
    expert_down,
    cotangent,
):
    ep_count = lax.axis_size("ep")
    row_count, model_width = tokens.shape
    heads_here, bias_part = query_bias.shape
    head_size = bias_part * ep_count
    heads_width = heads_here * head_size
    shared_hidden = shared_gate.shape[1]
    expert_hidden = expert_gate.shape[2]
    gain_part = norm_one_gain.shape[0]
    tp_at = lax.axis_index("tp")
    own_count = row_count // 4
    own_start = tp_at * own_count

    def own_rows(values):
        return lax.dynamic_slice_in_dim(values, own_start, own_count, 0)

    small = jnp.concatenate(
        [
            norm_one_gain,
            norm_two_gain,
            shared_switch,
            query_bias.reshape(-1),
            key_bias.reshape(-1),
            value_bias.reshape(-1),
        ]
    )
    full_qkv = ring_gather(jnp.concatenate([query_weight, key_weight, value_weight], axis=1))
    output_turned = output_weight.T
    shared_in = jnp.concatenate([shared_gate, shared_up], axis=1)
    shared_out = shared_down.T
    full_output = ring_gather(output_turned)
    full_shared = ring_gather(shared_in)
    full_down = ring_gather(shared_out)
    small = to_ring(small_gather(small), 0)
    gain_one = small[:, :gain_part].reshape(-1).astype(jnp.float32)
    gain_two = small[:, gain_part : 2 * gain_part].reshape(-1).astype(jnp.float32)
    full_switch = small[:, 2 * gain_part : 3 * gain_part].reshape(-1)
    bias_all = (
        from_ring(small[:, 3 * gain_part :], 0)
        .reshape(ep_count, 3 * heads_here, bias_part)
        .transpose(1, 0, 2)
        .reshape(-1)
        .astype(jnp.float32)
    )

    group = -(-expert_hidden // 128) * 128
    spare = group - expert_hidden

    def padded(weight):
        return jnp.pad(weight, ((0, 0), (0, spare)))

    expert_own = jnp.concatenate([padded(expert_gate[0]), padded(expert_up[0])], axis=1)
    expert_own = to_ring(expert_own, 0)
    expert_last = to_ring(expert_down[0], 1)
    expert_in = jnp.concatenate(tp_pieces(expert_own), axis=1)
    expert_out = jnp.zeros((4 * group, model_width), jnp.bfloat16)
    for i, piece in enumerate(tp_pieces(expert_last)):
        expert_out = lax.dynamic_update_slice(expert_out, piece, (i * group, 0))

    def gate_columns(values):
        return [values[:, (2 * i) * group : (2 * i + 1) * group] for i in range(4)]

    def up_columns(values):
        return [values[:, (2 * i + 1) * group : (2 * i + 2) * group] for i in range(4)]

    score_scale = head_size ** (-0.5)
    length_now = lengths[0]
    valid_rows = jnp.arange(row_count) < length_now
    valid_float = valid_rows.astype(jnp.float32)[:, None]
    experts_total = ep_count
    top_count = routes.shape[1]
    capacity = row_count * top_count // experts_total
    slots_here = capacity // 4
    slot_rows = experts_total * slots_here
    kept, slots = slot_plan(routes, slot_order[0], valid_rows, experts_total, capacity)
    slots = slots - tp_at * slots_here
    taken = kept & (slots >= 0) & (slots < slots_here)
    target = jnp.where(taken, routes * slots_here + slots, -1)
    slot_ids = jnp.arange(slot_rows, dtype=jnp.int32)[:, None]
    select = jnp.zeros((slot_rows, row_count), jnp.float32)
    weighted = jnp.zeros((slot_rows, row_count), jnp.float32)
    for choice in range(top_count):
        hit = slot_ids == target[:, choice][None, :]
        select = jnp.where(hit, 1.0, select)
        weighted = jnp.where(hit, route_weights[:, choice][None, :], weighted)
    select, weighted = low(select), low(weighted)

    grad_low = to_ring(cotangent, 1)
    grad_low = jnp.where(valid_rows[:, None], grad_low, jnp.zeros_like(grad_low))
    grad_out = grad_low.astype(jnp.float32)
    grad_sent = low(times(weighted, grad_low))
    grad_sent = grad_sent.reshape(experts_total, slots_here, model_width)
    grad_arrived = exchange(after(grad_sent, full_qkv))
    grad_arrived = grad_arrived.reshape(slot_rows, model_width)

    tokens = to_ring(tokens, 1)
    inputs = tokens.astype(jnp.float32)
    factor_one = rms_factor(inputs)
    cosine, sine = rotary_tables(row_count, head_size)
    normed_one = low(inputs * factor_one * gain_one)
    qkv = times(normed_one, full_qkv) + bias_all
    query_pre, key_pre, value_pre = (
        by_head(qkv[:, i * heads_width : (i + 1) * heads_width], heads_here)
        for i in range(3)
    )
    queries = low(rotate_forward(query_pre, cosine, sine))
    keys_rot = low(rotate_forward(key_pre, cosine, sine))
    values = low(value_pre)
    scores = masked_scores(queries, keys_rot, length_now, score_scale)
    peak = jnp.max(scores, axis=-1, keepdims=True)
    raised = jnp.exp(scores - peak)
    totals = jnp.sum(raised, axis=-1, keepdims=True)
    probs = raised / totals
    log_total = peak + jnp.log(totals)
    attended = jnp.einsum("hts,hsd->htd", low(probs), values, preferred_element_type=jnp.float32)
    attended_low = low(side_by_side(attended))
    attn_part = low(times_transpose(attended_low, full_output))
    own_inputs = own_rows(tokens).astype(jnp.float32)
    hidden = own_inputs + rows_scatter(attn_part)[0]
    factor_two = rms_factor(hidden)
    own_normed_two = low(hidden * factor_two * gain_two)
    normed_two = rows_gather(own_normed_two)

    sent = low(times(select, normed_two)).reshape(experts_total, slots_here, model_width)
    arrived = exchange(after(sent, grad_arrived)).reshape(slot_rows, model_width)
    act = times(arrived, expert_in)
    gate_act = jnp.concatenate(gate_columns(act), axis=1)
    up_act = jnp.concatenate(up_columns(act), axis=1)
    sigma = jax.nn.sigmoid(gate_act)
    swish = gate_act * sigma
    inner_act = low(swish * up_act)
    inner_grad = times_transpose(grad_arrived, expert_out)
    up_grad = low(inner_grad * swish)
    gate_grad = low(inner_grad * up_act * sigma * (1.0 + gate_act * (1.0 - sigma)))
    both_grad = jnp.concatenate(
        [part[:, i * group : (i + 1) * group] for i in range(4) for part in (gate_grad, up_grad)],
        axis=1,
    )
    back_rows = low(times_transpose(both_grad, expert_in))
    back_home = exchange(back_rows.reshape(experts_total, slots_here, model_width))
    back_home = back_home.reshape(slot_rows, model_width)
    both_last, inner_last = after((both_grad, inner_act), back_rows)
    grad_in = low(contract_rows(arrived, both_last))
    grad_in_terms, grad_in_sent = tp_reduce(
        [grad_in[:, 2 * i * group : 2 * (i + 1) * group] for i in range(4)]
    )
    inner_last = after(inner_last, grad_in)
    grad_down = low(contract_rows(inner_last, grad_arrived))
    grad_down_near = inner(
        jnp.stack([grad_down[i * group : i * group + expert_hidden] for i in (1, 3)])
    )
    produced = low(times(after(inner_last, grad_down), expert_out))
    produced_home = exchange(
        after(produced, back_home).reshape(experts_total, slots_here, model_width)
    )
    produced_home = produced_home.reshape(slot_rows, model_width)

    shared_rows = after(normed_two, produced, grad_in_sent)
    shared_act = times(shared_rows, full_shared)
    shared_gate_act = shared_act[:, :shared_hidden]
    shared_up_act = shared_act[:, shared_hidden:]
    shared_sigma = jax.nn.sigmoid(shared_gate_act)
    shared_swish = shared_gate_act * shared_sigma
    shared_inner = low(shared_swish * shared_up_act)
    switch_value = jax.nn.sigmoid(
        jnp.sum(shared_rows.astype(jnp.float32) * full_switch.astype(jnp.float32), axis=1)
    )
    shared_out_grad = low(switch_value[:, None] * grad_out)
    shared_inner_grad = times(shared_out_grad, full_down)
    shared_up_grad = low(shared_inner_grad * shared_swish)
    shared_gate_grad = low(
        shared_inner_grad
        * shared_up_act
        * shared_sigma
        * (1.0 + shared_gate_act * (1.0 - shared_sigma))
    )
    shared_grad = jnp.concatenate([shared_gate_grad, shared_up_grad], axis=1)
    shared_part_grad = low(contract_rows(shared_rows, shared_grad))
    grad_shared = ring_scatter(shared_part_grad)
    grad_shared_gate = grad_shared[:, :shared_hidden].astype(jnp.float32)
    grad_shared_up = grad_shared[:, shared_hidden:].astype(jnp.float32)
    shared_grad, select_then = after((shared_grad, select), shared_part_grad)
    normed_two_part = times_transpose(shared_grad, full_shared)
    normed_two_part = normed_two_part + contract_rows(select_then, back_home)
    normed_two_grad, normed_two_sent = rows_scatter(low(normed_two_part))
    shared_inner, shared_out_grad = after((shared_inner, shared_out_grad), normed_two_sent)
    shared_part = times_transpose(shared_inner, full_down)
    switch_total = jnp.sum(grad_out * shared_part, axis=1).reshape(-1, 128)
    switch_total = tp_sum(switch_total).reshape(-1)
    logit_grad = switch_total * switch_value * (1.0 - switch_value)

    own_logit_grad = own_rows(logit_grad)[:, None]
    normed_two_grad = normed_two_grad + own_logit_grad * full_switch.astype(jnp.float32)[None, :]
    switch_gradient = jnp.sum(own_logit_grad * own_normed_two.astype(jnp.float32), axis=0)
    second_gain_gradient = jnp.sum(normed_two_grad * hidden * factor_two, axis=0)
    scaled_two = normed_two_grad * gain_two
    hidden_grad = (
        own_rows(grad_out)
        + factor_two * scaled_two
        - hidden * factor_two**3 * jnp.mean(scaled_two * hidden, axis=-1, keepdims=True)
    )
    own_attn_grad = low(hidden_grad)
    attn_grad_low = rows_gather(own_attn_grad)

    grad_down, grad_down_near = after((grad_down, grad_down_near), attn_grad_low)
    grad_down_parts = [grad_down[i * group : i * group + expert_hidden] for i in (0, 2)]
    grad_down_far = outer(
        low(grad_down_parts[1].astype(jnp.float32) + grad_down_near[1].astype(jnp.float32))
    )
    grad_down_terms = (grad_down_parts[0], grad_down_near[0], grad_down_far)
    shared_out_grad = after(shared_out_grad, own_attn_grad)
    shared_down_part = low(contract_rows(shared_out_grad, shared_inner))
    grad_shared_down = ring_scatter(shared_down_part).T.astype(jnp.float32)
    attn_grad_low = after(attn_grad_low, shared_down_part)
    attended_flat = low(times(attn_grad_low, full_output))
    attended_grad = by_head(attended_flat, heads_here)
    scores_again = masked_scores(queries, keys_rot, length_now, score_scale)
    probs_again = jnp.exp(scores_again - log_total)
    value_grad = jnp.einsum(
        "hts,htd->hsd", low(probs_again), attended_grad, preferred_element_type=jnp.float32
    )
    probs_grad = jnp.einsum(
        "htd,hsd->hts", attended_grad, values, preferred_element_type=jnp.float32
    )
    row_dot = jnp.sum(probs_again * probs_grad, axis=-1, keepdims=True)
    score_grad = low(probs_again * (probs_grad - row_dot))
    query_grad = (
        jnp.einsum("hts,hsd->htd", score_grad, keys_rot, preferred_element_type=jnp.float32)
        * score_scale
    )
    key_grad = (
        jnp.einsum("hts,htd->hsd", score_grad, queries, preferred_element_type=jnp.float32)
        * score_scale
    )
    query_pre_grad = low(side_by_side(rotate_backward(query_grad, cosine, sine)))
    key_pre_grad = low(side_by_side(rotate_backward(key_grad, cosine, sine)))
    value_pre_grad = low(side_by_side(value_grad))
    qkv_grad = jnp.concatenate([query_pre_grad, key_pre_grad, value_pre_grad], axis=1)
    bias_grad = jnp.sum(qkv_grad.astype(jnp.float32), axis=0)
    mixed = contract_rows(weighted, produced_home) + switch_value[:, None] * shared_part
    mixed = after(low(mixed), attended_flat)
    own_valid = own_rows(valid_float)
    output = rows_gather(from_ring(low(own_valid * (hidden + rows_scatter(mixed)[0])), 1))

    qkv_part = contract_rows(normed_one, qkv_grad)
    qkv_grad = after(qkv_grad, qkv_part)
    normed_one_grad, _ = rows_scatter(low(times_transpose(qkv_grad, full_qkv)))
    grad_in_terms, grad_down_terms = after((grad_in_terms, grad_down_terms), qkv_part)
    grad_expert_gate = from_ring(add_terms([t[:, :expert_hidden] for t in grad_in_terms]), 0)[None]
    grad_expert_up = from_ring(
        add_terms([t[:, group : group + expert_hidden] for t in grad_in_terms]), 0
    )[None]
    grad_expert_down = from_ring(add_terms(grad_down_terms), 1)[None]
    own_factor = own_rows(factor_one)
    first_gain_gradient = jnp.sum(normed_one_grad * own_inputs * own_factor, axis=0)
    scaled_one = normed_one_grad * gain_one
    token_gradient = (
        hidden_grad
        + own_factor * scaled_one
        - own_inputs * own_factor**3 * jnp.mean(scaled_one * own_inputs, axis=-1, keepdims=True)
    )
    own_token_gradient = from_ring(low(token_gradient), 1)
    token_gradient = rows_gather(own_token_gradient)
    grad_qkv = ring_scatter(
        jnp.concatenate(
            [low(qkv_part), low(contract_rows(attn_grad_low, attended_low))], axis=1
        ),
    ).astype(jnp.float32)
    grad_output_weight = grad_qkv[:, 3 * heads_width :].T
    grad_query_weight, grad_key_weight, grad_value_weight = (
        grad_qkv[:, i * heads_width : (i + 1) * heads_width] for i in range(3)
    )

    row_sums = tp_sum(jnp.stack([first_gain_gradient, second_gain_gradient, switch_gradient]))
    small_grad = jnp.concatenate(
        [
            from_ring(
                row_sums.reshape(3, ep_count, gain_part).transpose(1, 0, 2).reshape(ep_count, -1),
                0,
            ),
            bias_grad.reshape(3 * heads_here, ep_count, bias_part)
            .transpose(1, 0, 2)
            .reshape(ep_count, -1),
        ],
        axis=1,
    )
    small_grad = small_scatter(small_grad)
    first_gain_gradient, second_gain_gradient, switch_gradient = (
        small_grad[i * gain_part : (i + 1) * gain_part] for i in range(3)
    )
    bias_size = heads_here * bias_part
    grad_query_bias, grad_key_bias, grad_value_bias = (
        small_grad[3 * gain_part + i * bias_size : 3 * gain_part + (i + 1) * bias_size].reshape(
            heads_here, bias_part
        )
        for i in range(3)
    )
    return (
        output,
        token_gradient,
        first_gain_gradient,
        grad_query_weight,
        grad_key_weight,
        grad_value_weight,
        grad_query_bias,
        grad_key_bias,
        grad_value_bias,
        grad_output_weight,
        second_gain_gradient,
        grad_shared_gate,
        grad_shared_up,
        grad_shared_down,
        switch_gradient,
        grad_expert_gate,
        grad_expert_up,
        grad_expert_down,
    )


def solution(mesh):
    in_specs = (
        P("ep", None),
        P("ep"),
        P("ep", None),
        P("ep", None),
        P("ep", None),
        P("ep"),
        P("ep", "tp"),
        P("ep", "tp"),
        P("ep", "tp"),
        P("tp", "ep"),
        P("tp", "ep"),
        P("tp", "ep"),
        P("tp", "ep"),
        P("ep"),
        P("ep", "tp"),
        P("ep", "tp"),
        P("tp", "ep"),
        P("ep"),
        P("ep", None, "tp"),
        P("ep", None, "tp"),
        P("ep", "tp", None),
        P("ep", None),
    )
    out_specs = (
        P("ep", None),
        P("ep", None),
        P("ep"),
        P("ep", "tp"),
        P("ep", "tp"),
        P("ep", "tp"),
        P("tp", "ep"),
        P("tp", "ep"),
        P("tp", "ep"),
        P("tp", "ep"),
        P("ep"),
        P("ep", "tp"),
        P("ep", "tp"),
        P("tp", "ep"),
        P("ep"),
        P("ep", None, "tp"),
        P("ep", None, "tp"),
        P("ep", "tp", None),
    )

    return jax.shard_map(body, mesh=mesh, in_specs=in_specs, out_specs=out_specs, check_vma=False)
```

```python
import jax
import jax.numpy as jnp
from jax import lax
from jax.sharding import PartitionSpec as P


norm_eps = 1e-06
rope_base = 1000000.0


def rms_factor(values):
    return lax.rsqrt(jnp.mean(values * values, axis=-1, keepdims=True) + norm_eps)


def rotary_tables(row_count, head_size):
    half_size = head_size // 2
    inverse = rope_base ** (-(jnp.arange(half_size, dtype=jnp.float32) * 2.0 / head_size))
    angles = jnp.arange(row_count, dtype=jnp.float32)[:, None] * inverse[None, :]
    cosine = jnp.concatenate([jnp.cos(angles), jnp.cos(angles)], axis=1)
    sine = jnp.concatenate([jnp.sin(angles), jnp.sin(angles)], axis=1)
    return (cosine[None], sine[None])


def rotate_forward(values, cosine, sine):
    half_size = values.shape[-1] // 2
    turned = jnp.concatenate([-values[..., half_size:], values[..., :half_size]], axis=-1)
    return values * cosine + turned * sine


def rotate_backward(grads, cosine, sine):
    half_size = grads.shape[-1] // 2
    scaled = grads * sine
    turned = jnp.concatenate([scaled[..., half_size:], -scaled[..., :half_size]], axis=-1)
    return grads * cosine + turned


def by_head(values, heads):
    size = values.shape[1] // heads
    return jnp.stack([values[:, h * size : (h + 1) * size] for h in range(heads)])


def side_by_side(values):
    return jnp.concatenate([values[h] for h in range(values.shape[0])], axis=1)


def times(left, right):
    return jnp.dot(left, right, preferred_element_type=jnp.float32)


def contract_rows(left, right):
    return lax.dot_general(
        left, right, (((0,), (0,)), ((), ())), preferred_element_type=jnp.float32
    )


def times_transpose(left, right):
    return lax.dot_general(
        left, right, (((1,), (1,)), ((), ())), preferred_element_type=jnp.float32
    )


def low(values):
    return values.astype(jnp.bfloat16)


def masked_scores(queries, keys, length_now, score_scale):
    scores = (
        jnp.einsum("htd,hsd->hts", queries, keys, preferred_element_type=jnp.float32) * score_scale
    )
    row_count = queries.shape[1]
    rows_at = jnp.arange(row_count)[:, None]
    cols_at = jnp.arange(row_count)[None, :]
    allowed = (cols_at <= rows_at) & (cols_at < length_now)
    return jnp.where(allowed[None], scores, -1e30)


def slot_plan(route_rows, rank_rows, valid_rows, experts_total, capacity):
    experts = jnp.arange(experts_total, dtype=jnp.int32)
    chosen = jnp.any(route_rows[:, :, None] == experts[None, None, :], axis=1)
    chosen = low(chosen & valid_rows[:, None])
    earlier = low(rank_rows[None, :] < rank_rows[:, None])
    counts = times(earlier, chosen).astype(jnp.int32)
    mine = route_rows[:, :, None] == experts[None, None, :]
    slots = jnp.sum(jnp.where(mine, counts[:, None, :], 0), axis=2)
    kept = valid_rows[:, None] & (slots < capacity)
    return (kept, slots)


def ring_order(count):
    return [*range(0, count, 2), *range(count - 1, 0, -2)]


def take_blocks(values, order, axis):
    size = values.shape[axis] // len(order)
    return jnp.concatenate(
        [lax.slice_in_dim(values, i * size, (i + 1) * size, axis=axis) for i in order], axis=axis
    )


def to_ring(values, axis):
    return take_blocks(values, ring_order(lax.axis_size("ep")), axis)


def from_ring(values, axis):
    order = ring_order(lax.axis_size("ep"))
    return take_blocks(values, [order.index(i) for i in range(len(order))], axis)


def ring_gather(shard):
    return lax.all_gather(
        shard, "ep", axis=0, tiled=True, axis_index_groups=[ring_order(lax.axis_size("ep"))]
    )


def ring_scatter(full):
    return lax.psum_scatter(
        full,
        "ep",
        scatter_dimension=0,
        tiled=True,
        axis_index_groups=[ring_order(lax.axis_size("ep"))],
    )


def mirror(values):
    count = lax.axis_size("ep")
    pairs = [(i, (i + count // 2) % count) for i in range(count)]
    return lax.ppermute(values, "ep", pairs)


def half_exchange(rows):
    count = lax.axis_size("ep")
    groups = [list(range(count // 2)), list(range(count // 2, count))]
    return lax.all_to_all(
        rows, "ep", split_axis=0, concat_axis=0, tiled=True, axis_index_groups=groups
    )


def after(values, *tokens):
    return lax.optimization_barrier((values, *tokens))[0]


def pair_up(values, distance):
    count = lax.axis_size("ep")
    return lax.ppermute(values, "ep", [(i, i ^ distance) for i in range(count)])


def small_gather(row):
    count = lax.axis_size("ep")
    index = lax.axis_index("ep")
    zero = jnp.zeros_like(index)
    full = jnp.broadcast_to(row[None], (count, row.shape[0]))
    distance = 1
    while distance < count:
        start = lax.div(index, distance) * distance
        other = start + distance - 2 * lax.rem(start, 2 * distance)
        block = lax.dynamic_slice(full, (start, zero), (distance, row.shape[0]))
        full = lax.dynamic_update_slice(full, pair_up(block, distance), (other, zero))
        distance *= 2
    return full


def small_scatter(rows):
    index = lax.axis_index("ep")
    distance = lax.axis_size("ep") // 2
    while distance >= 1:
        mine = lax.rem(lax.div(index, distance), 2)
        halves = rows.reshape(2, distance, rows.shape[1])
        kept = lax.dynamic_index_in_dim(halves, mine, 0, keepdims=False)
        sent = lax.dynamic_index_in_dim(halves, 1 - mine, 0, keepdims=False)
        rows = kept + pair_up(sent, distance)
        distance //= 2
    return rows[0]


def inner(values):
    return lax.ppermute(values, "tp", [(i, i ^ 1) for i in range(4)])


def outer(values):
    return lax.ppermute(values, "tp", [(i, i ^ 2) for i in range(4)])


def tp_place():
    member = lax.axis_index("tp")
    return lax.div(member, 2), lax.rem(member, 2)


def rows_scatter(partial):
    outer_at, inner_at = tp_place()
    rows, width = partial.shape
    split = partial.reshape(2, 2, rows // 4, width)
    arrived = inner(lax.dynamic_index_in_dim(split, 1 - inner_at, 1, keepdims=False))
    mine = lax.dynamic_index_in_dim(split, inner_at, 1, keepdims=False)
    summed = mine.astype(jnp.float32) + arrived.astype(jnp.float32)
    sent = low(lax.dynamic_index_in_dim(summed, 1 - outer_at, 0, keepdims=False))
    kept = lax.dynamic_index_in_dim(summed, outer_at, 0, keepdims=False)
    arrived = outer(sent)
    return kept + arrived.astype(jnp.float32), sent


def rows_gather(rows):
    outer_at, inner_at = tp_place()
    count, width = rows.shape
    across = outer(rows)
    beside = inner(rows)
    diagonal = inner(across)
    full = jnp.zeros((4 * count, width), rows.dtype)

    def put(full, piece, outer_now, inner_now):
        at = (outer_now * 2 + inner_now) * count
        return lax.dynamic_update_slice(full, piece, (at, jnp.zeros_like(at)))

    full = put(full, rows, outer_at, inner_at)
    full = put(full, beside, outer_at, 1 - inner_at)
    full = put(full, across, 1 - outer_at, inner_at)
    return put(full, diagonal, 1 - outer_at, 1 - inner_at)


def tp_pieces(own):
    across = outer(own)
    beside = inner(own)
    return [own, beside, across, inner(across)]


def tp_reduce(pieces):
    own, beside, across, diagonal = pieces
    near = inner(beside)
    sent = low(across.astype(jnp.float32) + inner(diagonal).astype(jnp.float32))
    far = outer(sent)
    return (own, near, far), sent


def add_terms(terms):
    own, near, far = (term.astype(jnp.float32) for term in terms)
    return own + near + far


def tp_sum(values):
    values = values + inner(values)
    return values + outer(values)


def exchange(rows):
    return lax.all_to_all(rows, "ep", split_axis=0, concat_axis=0, tiled=True)


def body(
    tokens,
    lengths,
    routes,
    route_weights,
    slot_order,
    norm_one_gain,
    query_weight,
    key_weight,
    value_weight,
    query_bias,
    key_bias,
    value_bias,
    output_weight,
    norm_two_gain,
    shared_gate,
    shared_up,
    shared_down,
    shared_switch,
    expert_gate,
    expert_up,
    expert_down,
    cotangent,
):
    ep_count = lax.axis_size("ep")
    row_count, model_width = tokens.shape
    heads_here, bias_part = query_bias.shape
    head_size = bias_part * ep_count
    heads_width = heads_here * head_size
    shared_hidden = shared_gate.shape[1]
    expert_hidden = expert_gate.shape[2]
    gain_part = norm_one_gain.shape[0]
    tp_at = lax.axis_index("tp")
    own_count = row_count // 4
    own_start = tp_at * own_count

    def own_rows(values):
        return lax.dynamic_slice_in_dim(values, own_start, own_count, 0)

    small = jnp.concatenate(
        [
            norm_one_gain,
            norm_two_gain,
            shared_switch,
            query_bias.reshape(-1),
            key_bias.reshape(-1),
            value_bias.reshape(-1),
        ]
    )
    full_qkv = ring_gather(jnp.concatenate([query_weight, key_weight, value_weight], axis=1))
    output_turned = output_weight.T
    shared_in = jnp.concatenate([shared_gate, shared_up], axis=1)
    shared_out = shared_down.T
    full_output = ring_gather(output_turned)
    full_shared = ring_gather(shared_in)
    full_down = ring_gather(shared_out)
    small = to_ring(small_gather(small), 0)
    gain_one = small[:, :gain_part].reshape(-1).astype(jnp.float32)
    gain_two = small[:, gain_part : 2 * gain_part].reshape(-1).astype(jnp.float32)
    full_switch = small[:, 2 * gain_part : 3 * gain_part].reshape(-1)
    bias_all = (
        from_ring(small[:, 3 * gain_part :], 0)
        .reshape(ep_count, 3 * heads_here, bias_part)
        .transpose(1, 0, 2)
        .reshape(-1)
        .astype(jnp.float32)
    )

    group = -(-expert_hidden // 128) * 128
    spare = group - expert_hidden

    def padded(weight):
        return jnp.pad(weight, ((0, 0), (0, spare)))

    expert_own = jnp.concatenate([padded(expert_gate[0]), padded(expert_up[0])], axis=1)
    expert_own = to_ring(expert_own, 0)
    expert_last = to_ring(expert_down[0], 1)
    expert_in = jnp.concatenate(tp_pieces(expert_own), axis=1)
    expert_out = jnp.zeros((4 * group, model_width), jnp.bfloat16)
    for i, piece in enumerate(tp_pieces(expert_last)):
        expert_out = lax.dynamic_update_slice(expert_out, piece, (i * group, 0))

    def gate_columns(values):
        return [values[:, (2 * i) * group : (2 * i + 1) * group] for i in range(4)]

    def up_columns(values):
        return [values[:, (2 * i + 1) * group : (2 * i + 2) * group] for i in range(4)]

    score_scale = head_size ** (-0.5)
    length_now = lengths[0]
    valid_rows = jnp.arange(row_count) < length_now
    valid_float = valid_rows.astype(jnp.float32)[:, None]
    experts_total = ep_count
    top_count = routes.shape[1]
    capacity = row_count * top_count // experts_total
    slots_here = capacity // 4
    slot_rows = experts_total * slots_here
    kept, slots = slot_plan(routes, slot_order[0], valid_rows, experts_total, capacity)
    slots = slots - tp_at * slots_here
    taken = kept & (slots >= 0) & (slots < slots_here)
    target = jnp.where(taken, routes * slots_here + slots, -1)
    slot_ids = jnp.arange(slot_rows, dtype=jnp.int32)[:, None]
    select = jnp.zeros((slot_rows, row_count), jnp.float32)
    weighted = jnp.zeros((slot_rows, row_count), jnp.float32)
    for choice in range(top_count):
        hit = slot_ids == target[:, choice][None, :]
        select = jnp.where(hit, 1.0, select)
        weighted = jnp.where(hit, route_weights[:, choice][None, :], weighted)
    select, weighted = low(select), low(weighted)

    half_count = ep_count // 2
    upper = lax.axis_index("ep") >= half_count
    half_slots = half_count * slots_here
    here = jnp.where(upper, half_slots, 0)
    half_ids = jnp.arange(half_slots, dtype=jnp.int32)[:, None] + here
    mirror_target = mirror(target)
    mirror_weights = mirror(route_weights)

    def in_order(own, other):
        return jnp.where(upper, other, own), jnp.where(upper, own, other)

    picks = []
    for targets, weights in zip(
        in_order(target, mirror_target), in_order(route_weights, mirror_weights)
    ):
        pick = jnp.zeros((half_slots, row_count), jnp.float32)
        for choice in range(top_count):
            hit = half_ids == targets[:, choice][None, :]
            pick = jnp.where(hit, weights[:, choice][None, :], pick)
        picks.append(low(pick))

    def packed(own, other):
        blocks = [
            low(times(pick, rows)).reshape(half_count, 1, slots_here, model_width)
            for pick, rows in zip(picks, in_order(own, other))
        ]
        return jnp.concatenate(blocks, axis=1)

    def by_block(rows):
        rows = rows.reshape(half_count, 2, slots_here, model_width)
        return rows.transpose(1, 0, 2, 3).reshape(experts_total, slots_here, model_width)

    grad_low = to_ring(cotangent, 1)
    grad_low = jnp.where(valid_rows[:, None], grad_low, jnp.zeros_like(grad_low))
    grad_out = grad_low.astype(jnp.float32)
    mirror_grad = rows_gather(mirror(after(own_rows(grad_low), full_qkv)))
    grad_sent = packed(grad_low, mirror_grad)
    grad_arrived = by_block(half_exchange(grad_sent)).reshape(slot_rows, model_width)

    tokens = to_ring(tokens, 1)
    inputs = tokens.astype(jnp.float32)
    factor_one = rms_factor(inputs)
    cosine, sine = rotary_tables(row_count, head_size)
    normed_one = low(inputs * factor_one * gain_one)
    qkv = times(normed_one, full_qkv) + bias_all
    query_pre, key_pre, value_pre = (
        by_head(qkv[:, i * heads_width : (i + 1) * heads_width], heads_here)
        for i in range(3)
    )
    queries = low(rotate_forward(query_pre, cosine, sine))
    keys_rot = low(rotate_forward(key_pre, cosine, sine))
    values = low(value_pre)
    scores = masked_scores(queries, keys_rot, length_now, score_scale)
    peak = jnp.max(scores, axis=-1, keepdims=True)
    raised = jnp.exp(scores - peak)
    totals = jnp.sum(raised, axis=-1, keepdims=True)
    probs = raised / totals
    log_total = peak + jnp.log(totals)
    attended = jnp.einsum("hts,hsd->htd", low(probs), values, preferred_element_type=jnp.float32)
    attended_low = low(side_by_side(attended))
    attn_part = low(times_transpose(attended_low, full_output))
    own_inputs = own_rows(tokens).astype(jnp.float32)
    hidden = own_inputs + rows_scatter(attn_part)[0]
    factor_two = rms_factor(hidden)
    own_normed_two = low(hidden * factor_two * gain_two)
    normed_two = rows_gather(own_normed_two)

    sent = low(times(select, normed_two)).reshape(experts_total, slots_here, model_width)
    arrived = exchange(after(sent, grad_arrived)).reshape(slot_rows, model_width)
    act = times(arrived, expert_in)
    gate_act = jnp.concatenate(gate_columns(act), axis=1)
    up_act = jnp.concatenate(up_columns(act), axis=1)
    sigma = jax.nn.sigmoid(gate_act)
    swish = gate_act * sigma
    inner_act = low(swish * up_act)
    inner_grad = times_transpose(grad_arrived, expert_out)
    up_grad = low(inner_grad * swish)
    gate_grad = low(inner_grad * up_act * sigma * (1.0 + gate_act * (1.0 - sigma)))
    both_grad = jnp.concatenate(
        [part[:, i * group : (i + 1) * group] for i in range(4) for part in (gate_grad, up_grad)],
        axis=1,
    )
    back_rows = low(times_transpose(both_grad, expert_in))
    back_home = exchange(back_rows.reshape(experts_total, slots_here, model_width))
    back_home = back_home.reshape(slot_rows, model_width)
    both_last, inner_last = after((both_grad, inner_act), back_rows)
    grad_in = low(contract_rows(arrived, both_last))
    grad_in_terms, _ = tp_reduce(
        [grad_in[:, 2 * i * group : 2 * (i + 1) * group] for i in range(4)]
    )

    shared_rows = after(normed_two, grad_in)
    shared_act = times(shared_rows, full_shared)
    shared_gate_act = shared_act[:, :shared_hidden]
    shared_up_act = shared_act[:, shared_hidden:]
    shared_sigma = jax.nn.sigmoid(shared_gate_act)
    shared_swish = shared_gate_act * shared_sigma
    shared_inner = low(shared_swish * shared_up_act)
    switch_value = jax.nn.sigmoid(
        jnp.sum(shared_rows.astype(jnp.float32) * full_switch.astype(jnp.float32), axis=1)
    )
    shared_out_grad = low(switch_value[:, None] * grad_out)
    shared_inner_grad = times(shared_out_grad, full_down)
    shared_up_grad = low(shared_inner_grad * shared_swish)
    shared_gate_grad = low(
        shared_inner_grad
        * shared_up_act
        * shared_sigma
        * (1.0 + shared_gate_act * (1.0 - shared_sigma))
    )
    shared_grad = jnp.concatenate([shared_gate_grad, shared_up_grad], axis=1)
    shared_part_grad = low(contract_rows(shared_rows, shared_grad))
    grad_shared = ring_scatter(shared_part_grad)
    inner_last = after(inner_last, shared_part_grad)
    grad_down = low(contract_rows(inner_last, grad_arrived))
    grad_down_near = inner(
        jnp.stack([grad_down[i * group : i * group + expert_hidden] for i in (1, 3)])
    )
    produced = low(times(after(inner_last, grad_down), expert_out))
    produced_home = exchange(
        after(produced, back_home).reshape(experts_total, slots_here, model_width)
    )
    produced_home = produced_home.reshape(slot_rows, model_width)
    grad_shared_gate = grad_shared[:, :shared_hidden].astype(jnp.float32)
    grad_shared_up = grad_shared[:, shared_hidden:].astype(jnp.float32)
    shared_grad, select_then = after((shared_grad, select), shared_part_grad)
    normed_two_part = times_transpose(shared_grad, full_shared)
    normed_two_part = normed_two_part + contract_rows(select_then, back_home)
    normed_two_grad, normed_two_sent = rows_scatter(low(normed_two_part))
    shared_inner, shared_out_grad = after((shared_inner, shared_out_grad), normed_two_sent)
    shared_part = times_transpose(shared_inner, full_down)
    switch_total = jnp.sum(grad_out * shared_part, axis=1).reshape(-1, 128)
    switch_total = tp_sum(switch_total).reshape(-1)
    logit_grad = switch_total * switch_value * (1.0 - switch_value)

    own_logit_grad = own_rows(logit_grad)[:, None]
    normed_two_grad = normed_two_grad + own_logit_grad * full_switch.astype(jnp.float32)[None, :]
    switch_gradient = jnp.sum(own_logit_grad * own_normed_two.astype(jnp.float32), axis=0)
    second_gain_gradient = jnp.sum(normed_two_grad * hidden * factor_two, axis=0)
    scaled_two = normed_two_grad * gain_two
    hidden_grad = (
        own_rows(grad_out)
        + factor_two * scaled_two
        - hidden * factor_two**3 * jnp.mean(scaled_two * hidden, axis=-1, keepdims=True)
    )
    own_attn_grad = low(hidden_grad)
    attn_grad_low = rows_gather(own_attn_grad)

    grad_down, grad_down_near = after((grad_down, grad_down_near), attn_grad_low)
    grad_down_parts = [grad_down[i * group : i * group + expert_hidden] for i in (0, 2)]
    grad_down_far = outer(
        low(grad_down_parts[1].astype(jnp.float32) + grad_down_near[1].astype(jnp.float32))
    )
    grad_down_terms = (grad_down_parts[0], grad_down_near[0], grad_down_far)
    shared_out_grad = after(shared_out_grad, own_attn_grad)
    shared_down_part = low(contract_rows(shared_out_grad, shared_inner))
    grad_shared_down = ring_scatter(shared_down_part).T.astype(jnp.float32)
    attn_grad_low = after(attn_grad_low, shared_down_part)
    attended_flat = low(times(attn_grad_low, full_output))
    attended_grad = by_head(attended_flat, heads_here)
    scores_again = masked_scores(queries, keys_rot, length_now, score_scale)
    probs_again = jnp.exp(scores_again - log_total)
    value_grad = jnp.einsum(
        "hts,htd->hsd", low(probs_again), attended_grad, preferred_element_type=jnp.float32
    )
    probs_grad = jnp.einsum(
        "htd,hsd->hts", attended_grad, values, preferred_element_type=jnp.float32
    )
    row_dot = jnp.sum(probs_again * probs_grad, axis=-1, keepdims=True)
    score_grad = low(probs_again * (probs_grad - row_dot))
    query_grad = (
        jnp.einsum("hts,hsd->htd", score_grad, keys_rot, preferred_element_type=jnp.float32)
        * score_scale
    )
    key_grad = (
        jnp.einsum("hts,htd->hsd", score_grad, queries, preferred_element_type=jnp.float32)
        * score_scale
    )
    query_pre_grad = low(side_by_side(rotate_backward(query_grad, cosine, sine)))
    key_pre_grad = low(side_by_side(rotate_backward(key_grad, cosine, sine)))
    value_pre_grad = low(side_by_side(value_grad))
    qkv_grad = jnp.concatenate([query_pre_grad, key_pre_grad, value_pre_grad], axis=1)
    bias_grad = jnp.sum(qkv_grad.astype(jnp.float32), axis=0)
    mixed = contract_rows(weighted, produced_home) + switch_value[:, None] * shared_part
    mixed = after(low(mixed), attended_flat)
    own_valid = own_rows(valid_float)
    output = rows_gather(from_ring(low(own_valid * (hidden + rows_scatter(mixed)[0])), 1))

    qkv_part = contract_rows(normed_one, qkv_grad)
    qkv_grad = after(qkv_grad, qkv_part)
    normed_one_grad, _ = rows_scatter(low(times_transpose(qkv_grad, full_qkv)))
    grad_in_terms, grad_down_terms = after((grad_in_terms, grad_down_terms), qkv_part)
    grad_expert_gate = from_ring(add_terms([t[:, :expert_hidden] for t in grad_in_terms]), 0)[None]
    grad_expert_up = from_ring(
        add_terms([t[:, group : group + expert_hidden] for t in grad_in_terms]), 0
    )[None]
    grad_expert_down = from_ring(add_terms(grad_down_terms), 1)[None]
    own_factor = own_rows(factor_one)
    first_gain_gradient = jnp.sum(normed_one_grad * own_inputs * own_factor, axis=0)
    scaled_one = normed_one_grad * gain_one
    token_gradient = (
        hidden_grad
        + own_factor * scaled_one
        - own_inputs * own_factor**3 * jnp.mean(scaled_one * own_inputs, axis=-1, keepdims=True)
    )
    own_token_gradient = from_ring(low(token_gradient), 1)
    token_gradient = rows_gather(own_token_gradient)
    grad_qkv = ring_scatter(
        jnp.concatenate(
            [low(qkv_part), low(contract_rows(attn_grad_low, attended_low))], axis=1
        ),
    ).astype(jnp.float32)
    grad_output_weight = grad_qkv[:, 3 * heads_width :].T
    grad_query_weight, grad_key_weight, grad_value_weight = (
        grad_qkv[:, i * heads_width : (i + 1) * heads_width] for i in range(3)
    )

    row_sums = tp_sum(jnp.stack([first_gain_gradient, second_gain_gradient, switch_gradient]))
    small_grad = jnp.concatenate(
        [
            from_ring(
                row_sums.reshape(3, ep_count, gain_part).transpose(1, 0, 2).reshape(ep_count, -1),
                0,
            ),
            bias_grad.reshape(3 * heads_here, ep_count, bias_part)
            .transpose(1, 0, 2)
            .reshape(ep_count, -1),
        ],
        axis=1,
    )
    small_grad = small_scatter(small_grad)
    first_gain_gradient, second_gain_gradient, switch_gradient = (
        small_grad[i * gain_part : (i + 1) * gain_part] for i in range(3)
    )
    bias_size = heads_here * bias_part
    grad_query_bias, grad_key_bias, grad_value_bias = (
        small_grad[3 * gain_part + i * bias_size : 3 * gain_part + (i + 1) * bias_size].reshape(
            heads_here, bias_part
        )
        for i in range(3)
    )
    return (
        output,
        token_gradient,
        first_gain_gradient,
        grad_query_weight,
        grad_key_weight,
        grad_value_weight,
        grad_query_bias,
        grad_key_bias,
        grad_value_bias,
        grad_output_weight,
        second_gain_gradient,
        grad_shared_gate,
        grad_shared_up,
        grad_shared_down,
        switch_gradient,
        grad_expert_gate,
        grad_expert_up,
        grad_expert_down,
    )


def solution(mesh):
    in_specs = (
        P("ep", None),
        P("ep"),
        P("ep", None),
        P("ep", None),
        P("ep", None),
        P("ep"),
        P("ep", "tp"),
        P("ep", "tp"),
        P("ep", "tp"),
        P("tp", "ep"),
        P("tp", "ep"),
        P("tp", "ep"),
        P("tp", "ep"),
        P("ep"),
        P("ep", "tp"),
        P("ep", "tp"),
        P("tp", "ep"),
        P("ep"),
        P("ep", None, "tp"),
        P("ep", None, "tp"),
        P("ep", "tp", None),
        P("ep", None),
    )
    out_specs = (
        P("ep", None),
        P("ep", None),
        P("ep"),
        P("ep", "tp"),
        P("ep", "tp"),
        P("ep", "tp"),
        P("tp", "ep"),
        P("tp", "ep"),
        P("tp", "ep"),
        P("tp", "ep"),
        P("ep"),
        P("ep", "tp"),
        P("ep", "tp"),
        P("tp", "ep"),
        P("ep"),
        P("ep", None, "tp"),
        P("ep", None, "tp"),
        P("ep", "tp", None),
    )

    return jax.shard_map(body, mesh=mesh, in_specs=in_specs, out_specs=out_specs, check_vma=False)
```

```python
import jax
import jax.numpy as jnp
from jax import lax
from jax.sharding import PartitionSpec as P


norm_eps = 1e-06
rope_base = 1000000.0


def rms_factor(values):
    return lax.rsqrt(jnp.mean(values * values, axis=-1, keepdims=True) + norm_eps)


def rotary_tables(row_count, head_size):
    half_size = head_size // 2
    inverse = rope_base ** (-(jnp.arange(half_size, dtype=jnp.float32) * 2.0 / head_size))
    angles = jnp.arange(row_count, dtype=jnp.float32)[:, None] * inverse[None, :]
    cosine = jnp.concatenate([jnp.cos(angles), jnp.cos(angles)], axis=1)
    sine = jnp.concatenate([jnp.sin(angles), jnp.sin(angles)], axis=1)
    return (cosine[None], sine[None])


def rotate_forward(values, cosine, sine):
    half_size = values.shape[-1] // 2
    turned = jnp.concatenate([-values[..., half_size:], values[..., :half_size]], axis=-1)
    return values * cosine + turned * sine


def rotate_backward(grads, cosine, sine):
    half_size = grads.shape[-1] // 2
    scaled = grads * sine
    turned = jnp.concatenate([scaled[..., half_size:], -scaled[..., :half_size]], axis=-1)
    return grads * cosine + turned


def by_head(values, heads):
    size = values.shape[1] // heads
    return jnp.stack([values[:, h * size : (h + 1) * size] for h in range(heads)])


def side_by_side(values):
    return jnp.concatenate([values[h] for h in range(values.shape[0])], axis=1)


def times(left, right):
    return jnp.dot(left, right, preferred_element_type=jnp.float32)


def contract_rows(left, right):
    return lax.dot_general(
        left, right, (((0,), (0,)), ((), ())), preferred_element_type=jnp.float32
    )


def times_transpose(left, right):
    return lax.dot_general(
        left, right, (((1,), (1,)), ((), ())), preferred_element_type=jnp.float32
    )


def low(values):
    return values.astype(jnp.bfloat16)


def masked_scores(queries, keys, length_now, score_scale):
    scores = (
        jnp.einsum("htd,hsd->hts", queries, keys, preferred_element_type=jnp.float32) * score_scale
    )
    row_count = queries.shape[1]
    rows_at = jnp.arange(row_count)[:, None]
    cols_at = jnp.arange(row_count)[None, :]
    allowed = (cols_at <= rows_at) & (cols_at < length_now)
    return jnp.where(allowed[None], scores, -1e30)


def slot_plan(route_rows, rank_rows, valid_rows, experts_total, capacity):
    experts = jnp.arange(experts_total, dtype=jnp.int32)
    chosen = jnp.any(route_rows[:, :, None] == experts[None, None, :], axis=1)
    chosen = low(chosen & valid_rows[:, None])
    earlier = low(rank_rows[None, :] < rank_rows[:, None])
    counts = times(earlier, chosen).astype(jnp.int32)
    mine = route_rows[:, :, None] == experts[None, None, :]
    slots = jnp.sum(jnp.where(mine, counts[:, None, :], 0), axis=2)
    kept = valid_rows[:, None] & (slots < capacity)
    return (kept, slots)


def ring_order(count):
    return [*range(0, count, 2), *range(count - 1, 0, -2)]


def take_blocks(values, order, axis):
    size = values.shape[axis] // len(order)
    return jnp.concatenate(
        [lax.slice_in_dim(values, i * size, (i + 1) * size, axis=axis) for i in order], axis=axis
    )


def to_ring(values, axis):
    return take_blocks(values, ring_order(lax.axis_size("ep")), axis)


def from_ring(values, axis):
    order = ring_order(lax.axis_size("ep"))
    return take_blocks(values, [order.index(i) for i in range(len(order))], axis)


def ring_gather(shard):
    return lax.all_gather(
        shard, "ep", axis=0, tiled=True, axis_index_groups=[ring_order(lax.axis_size("ep"))]
    )


def ring_scatter(full):
    return lax.psum_scatter(
        full,
        "ep",
        scatter_dimension=0,
        tiled=True,
        axis_index_groups=[ring_order(lax.axis_size("ep"))],
    )


def mirror(values):
    count = lax.axis_size("ep")
    pairs = [(i, (i + count // 2) % count) for i in range(count)]
    return lax.ppermute(values, "ep", pairs)


def half_exchange(rows):
    count = lax.axis_size("ep")
    groups = [list(range(count // 2)), list(range(count // 2, count))]
    return lax.all_to_all(
        rows, "ep", split_axis=0, concat_axis=0, tiled=True, axis_index_groups=groups
    )


def after(values, *tokens):
    return lax.optimization_barrier((values, *tokens))[0]


def pair_up(values, distance):
    count = lax.axis_size("ep")
    return lax.ppermute(values, "ep", [(i, i ^ distance) for i in range(count)])


def small_gather(row):
    count = lax.axis_size("ep")
    index = lax.axis_index("ep")
    zero = jnp.zeros_like(index)
    full = jnp.broadcast_to(row[None], (count, row.shape[0]))
    distance = 1
    while distance < count:
        start = lax.div(index, distance) * distance
        other = start + distance - 2 * lax.rem(start, 2 * distance)
        block = lax.dynamic_slice(full, (start, zero), (distance, row.shape[0]))
        full = lax.dynamic_update_slice(full, pair_up(block, distance), (other, zero))
        distance *= 2
    return full


def small_scatter(rows):
    index = lax.axis_index("ep")
    distance = lax.axis_size("ep") // 2
    while distance >= 1:
        mine = lax.rem(lax.div(index, distance), 2)
        halves = rows.reshape(2, distance, rows.shape[1])
        kept = lax.dynamic_index_in_dim(halves, mine, 0, keepdims=False)
        sent = lax.dynamic_index_in_dim(halves, 1 - mine, 0, keepdims=False)
        rows = kept + pair_up(sent, distance)
        distance //= 2
    return rows[0]


def inner(values):
    return lax.ppermute(values, "tp", [(i, i ^ 1) for i in range(4)])


def outer(values):
    return lax.ppermute(values, "tp", [(i, i ^ 2) for i in range(4)])


def tp_place():
    member = lax.axis_index("tp")
    return lax.div(member, 2), lax.rem(member, 2)


def rows_scatter(partial):
    outer_at, inner_at = tp_place()
    rows, width = partial.shape
    split = partial.reshape(2, 2, rows // 4, width)
    arrived = inner(lax.dynamic_index_in_dim(split, 1 - inner_at, 1, keepdims=False))
    mine = lax.dynamic_index_in_dim(split, inner_at, 1, keepdims=False)
    summed = mine.astype(jnp.float32) + arrived.astype(jnp.float32)
    sent = low(lax.dynamic_index_in_dim(summed, 1 - outer_at, 0, keepdims=False))
    kept = lax.dynamic_index_in_dim(summed, outer_at, 0, keepdims=False)
    arrived = outer(sent)
    return kept + arrived.astype(jnp.float32), sent


def rows_gather(rows):
    outer_at, inner_at = tp_place()
    count, width = rows.shape
    across = outer(rows)
    beside = inner(rows)
    diagonal = inner(across)
    full = jnp.zeros((4 * count, width), rows.dtype)

    def put(full, piece, outer_now, inner_now):
        at = (outer_now * 2 + inner_now) * count
        return lax.dynamic_update_slice(full, piece, (at, jnp.zeros_like(at)))

    full = put(full, rows, outer_at, inner_at)
    full = put(full, beside, outer_at, 1 - inner_at)
    full = put(full, across, 1 - outer_at, inner_at)
    return put(full, diagonal, 1 - outer_at, 1 - inner_at)


def tp_pieces(own):
    across = outer(own)
    beside = inner(own)
    return [own, beside, across, inner(across)]


def tp_reduce(pieces):
    own, beside, across, diagonal = pieces
    near = inner(beside)
    sent = low(across.astype(jnp.float32) + inner(diagonal).astype(jnp.float32))
    far = outer(sent)
    return (own, near, far), sent


def add_terms(terms):
    own, near, far = (term.astype(jnp.float32) for term in terms)
    return own + near + far


def tp_sum(values):
    values = values + inner(values)
    return values + outer(values)


def exchange(rows):
    return lax.all_to_all(rows, "ep", split_axis=0, concat_axis=0, tiled=True)


def body(
    tokens,
    lengths,
    routes,
    route_weights,
    slot_order,
    norm_one_gain,
    query_weight,
    key_weight,
    value_weight,
    query_bias,
    key_bias,
    value_bias,
    output_weight,
    norm_two_gain,
    shared_gate,
    shared_up,
    shared_down,
    shared_switch,
    expert_gate,
    expert_up,
    expert_down,
    cotangent,
):
    ep_count = lax.axis_size("ep")
    row_count, model_width = tokens.shape
    heads_here, bias_part = query_bias.shape
    head_size = bias_part * ep_count
    heads_width = heads_here * head_size
    shared_hidden = shared_gate.shape[1]
    expert_hidden = expert_gate.shape[2]
    gain_part = norm_one_gain.shape[0]
    tp_at = lax.axis_index("tp")
    own_count = row_count // 4
    own_start = tp_at * own_count

    def own_rows(values):
        return lax.dynamic_slice_in_dim(values, own_start, own_count, 0)

    small = jnp.concatenate(
        [
            norm_one_gain,
            norm_two_gain,
            shared_switch,
            query_bias.reshape(-1),
            key_bias.reshape(-1),
            value_bias.reshape(-1),
        ]
    )
    full_qkv = ring_gather(jnp.concatenate([query_weight, key_weight, value_weight], axis=1))
    output_turned = output_weight.T
    shared_in = jnp.concatenate([shared_gate, shared_up], axis=1)
    shared_out = shared_down.T
    full_output = ring_gather(output_turned)
    full_shared = ring_gather(shared_in)
    full_down = ring_gather(shared_out)
    small = to_ring(small_gather(small), 0)
    gain_one = small[:, :gain_part].reshape(-1).astype(jnp.float32)
    gain_two = small[:, gain_part : 2 * gain_part].reshape(-1).astype(jnp.float32)
    full_switch = small[:, 2 * gain_part : 3 * gain_part].reshape(-1)
    bias_all = (
        from_ring(small[:, 3 * gain_part :], 0)
        .reshape(ep_count, 3 * heads_here, bias_part)
        .transpose(1, 0, 2)
        .reshape(-1)
        .astype(jnp.float32)
    )

    group = -(-expert_hidden // 128) * 128
    spare = group - expert_hidden

    def padded(weight):
        return jnp.pad(weight, ((0, 0), (0, spare)))

    expert_own = jnp.concatenate([padded(expert_gate[0]), padded(expert_up[0])], axis=1)
    expert_own = to_ring(expert_own, 0)
    expert_last = to_ring(expert_down[0], 1)
    expert_in = jnp.concatenate(tp_pieces(expert_own), axis=1)
    expert_out = jnp.zeros((4 * group, model_width), jnp.bfloat16)
    for i, piece in enumerate(tp_pieces(expert_last)):
        expert_out = lax.dynamic_update_slice(expert_out, piece, (i * group, 0))

    def gate_columns(values):
        return [values[:, (2 * i) * group : (2 * i + 1) * group] for i in range(4)]

    def up_columns(values):
        return [values[:, (2 * i + 1) * group : (2 * i + 2) * group] for i in range(4)]

    score_scale = head_size ** (-0.5)
    length_now = lengths[0]
    valid_rows = jnp.arange(row_count) < length_now
    valid_float = valid_rows.astype(jnp.float32)[:, None]
    experts_total = ep_count
    top_count = routes.shape[1]
    capacity = row_count * top_count // experts_total
    slots_here = capacity // 4
    slot_rows = experts_total * slots_here
    kept, slots = slot_plan(routes, slot_order[0], valid_rows, experts_total, capacity)
    slots = slots - tp_at * slots_here
    taken = kept & (slots >= 0) & (slots < slots_here)
    target = jnp.where(taken, routes * slots_here + slots, -1)
    slot_ids = jnp.arange(slot_rows, dtype=jnp.int32)[:, None]
    select = jnp.zeros((slot_rows, row_count), jnp.float32)
    weighted = jnp.zeros((slot_rows, row_count), jnp.float32)
    for choice in range(top_count):
        hit = slot_ids == target[:, choice][None, :]
        select = jnp.where(hit, 1.0, select)
        weighted = jnp.where(hit, route_weights[:, choice][None, :], weighted)
    select, weighted = low(select), low(weighted)

    half_count = ep_count // 2
    upper = lax.axis_index("ep") >= half_count
    half_slots = half_count * slots_here
    here = jnp.where(upper, half_slots, 0)
    half_ids = jnp.arange(half_slots, dtype=jnp.int32)[:, None] + here
    mirror_target = mirror(target)
    mirror_weights = mirror(route_weights)

    def in_order(own, other):
        return jnp.where(upper, other, own), jnp.where(upper, own, other)

    picks = []
    for targets, weights in zip(
        in_order(target, mirror_target), in_order(route_weights, mirror_weights)
    ):
        pick = jnp.zeros((half_slots, row_count), jnp.float32)
        for choice in range(top_count):
            hit = half_ids == targets[:, choice][None, :]
            pick = jnp.where(hit, weights[:, choice][None, :], pick)
        picks.append(low(pick))

    def packed(own, other):
        blocks = [
            low(times(pick, rows)).reshape(half_count, 1, slots_here, model_width)
            for pick, rows in zip(picks, in_order(own, other))
        ]
        return jnp.concatenate(blocks, axis=1)

    def by_block(rows):
        rows = rows.reshape(half_count, 2, slots_here, model_width)
        return rows.transpose(1, 0, 2, 3).reshape(experts_total, slots_here, model_width)

    grad_low = to_ring(cotangent, 1)
    grad_low = jnp.where(valid_rows[:, None], grad_low, jnp.zeros_like(grad_low))
    grad_out = grad_low.astype(jnp.float32)
    mirror_grad = rows_gather(mirror(after(own_rows(grad_low), full_qkv)))
    grad_sent = packed(grad_low, mirror_grad)
    grad_arrived = by_block(half_exchange(grad_sent)).reshape(slot_rows, model_width)

    tokens = to_ring(tokens, 1)
    inputs = tokens.astype(jnp.float32)
    factor_one = rms_factor(inputs)
    cosine, sine = rotary_tables(row_count, head_size)
    normed_one = low(inputs * factor_one * gain_one)
    qkv = times(normed_one, full_qkv) + bias_all
    query_pre, key_pre, value_pre = (
        by_head(qkv[:, i * heads_width : (i + 1) * heads_width], heads_here)
        for i in range(3)
    )
    queries = low(rotate_forward(query_pre, cosine, sine))
    keys_rot = low(rotate_forward(key_pre, cosine, sine))
    values = low(value_pre)
    scores = masked_scores(queries, keys_rot, length_now, score_scale)
    peak = jnp.max(scores, axis=-1, keepdims=True)
    raised = jnp.exp(scores - peak)
    totals = jnp.sum(raised, axis=-1, keepdims=True)
    probs = raised / totals
    log_total = peak + jnp.log(totals)
    attended = jnp.einsum("hts,hsd->htd", low(probs), values, preferred_element_type=jnp.float32)
    attended_low = low(side_by_side(attended))
    attn_part = low(times_transpose(attended_low, full_output))
    own_inputs = own_rows(tokens).astype(jnp.float32)
    hidden = own_inputs + rows_scatter(attn_part)[0]
    factor_two = rms_factor(hidden)
    own_normed_two = low(hidden * factor_two * gain_two)
    normed_two = rows_gather(own_normed_two)

    sent = low(times(select, normed_two)).reshape(experts_total, slots_here, model_width)
    arrived = exchange(after(sent, grad_arrived)).reshape(slot_rows, model_width)
    act = times(arrived, expert_in)
    gate_act = jnp.concatenate(gate_columns(act), axis=1)
    up_act = jnp.concatenate(up_columns(act), axis=1)
    sigma = jax.nn.sigmoid(gate_act)
    swish = gate_act * sigma
    inner_act = low(swish * up_act)
    inner_grad = times_transpose(grad_arrived, expert_out)
    up_grad = low(inner_grad * swish)
    gate_grad = low(inner_grad * up_act * sigma * (1.0 + gate_act * (1.0 - sigma)))
    both_grad = jnp.concatenate(
        [part[:, i * group : (i + 1) * group] for i in range(4) for part in (gate_grad, up_grad)],
        axis=1,
    )
    back_rows = low(times_transpose(both_grad, expert_in))
    back_home = exchange(back_rows.reshape(experts_total, slots_here, model_width))
    back_home = back_home.reshape(slot_rows, model_width)
    shared_rows = after(normed_two, back_rows)
    shared_act = times(shared_rows, full_shared)
    shared_gate_act = shared_act[:, :shared_hidden]
    shared_up_act = shared_act[:, shared_hidden:]
    shared_sigma = jax.nn.sigmoid(shared_gate_act)
    shared_swish = shared_gate_act * shared_sigma
    shared_inner = low(shared_swish * shared_up_act)
    switch_value = jax.nn.sigmoid(
        jnp.sum(shared_rows.astype(jnp.float32) * full_switch.astype(jnp.float32), axis=1)
    )
    shared_out_grad = low(switch_value[:, None] * grad_out)
    shared_inner_grad = times(shared_out_grad, full_down)
    shared_up_grad = low(shared_inner_grad * shared_swish)
    shared_gate_grad = low(
        shared_inner_grad
        * shared_up_act
        * shared_sigma
        * (1.0 + shared_gate_act * (1.0 - shared_sigma))
    )
    shared_grad = jnp.concatenate([shared_gate_grad, shared_up_grad], axis=1)
    shared_part_grad = low(contract_rows(shared_rows, shared_grad))
    grad_shared = ring_scatter(shared_part_grad)
    both_last, inner_last = after((both_grad, inner_act), shared_part_grad)
    grad_in = low(contract_rows(arrived, both_last))
    grad_in_terms, _ = tp_reduce(
        [grad_in[:, 2 * i * group : 2 * (i + 1) * group] for i in range(4)]
    )

    inner_last = after(inner_last, grad_in)
    grad_down = low(contract_rows(inner_last, grad_arrived))
    grad_down_near = inner(
        jnp.stack([grad_down[i * group : i * group + expert_hidden] for i in (1, 3)])
    )
    produced = low(times(after(inner_last, grad_down), expert_out))
    produced_home = exchange(
        after(produced, back_home).reshape(experts_total, slots_here, model_width)
    )
    produced_home = produced_home.reshape(slot_rows, model_width)
    grad_shared_gate = grad_shared[:, :shared_hidden].astype(jnp.float32)
    grad_shared_up = grad_shared[:, shared_hidden:].astype(jnp.float32)
    shared_grad, select_then = after((shared_grad, select), shared_part_grad)
    normed_two_part = times_transpose(shared_grad, full_shared)
    normed_two_part = normed_two_part + contract_rows(select_then, back_home)
    normed_two_grad, normed_two_sent = rows_scatter(low(normed_two_part))
    shared_inner, shared_out_grad = after((shared_inner, shared_out_grad), normed_two_sent)
    shared_part = times_transpose(shared_inner, full_down)
    switch_total = jnp.sum(grad_out * shared_part, axis=1).reshape(-1, 128)
    switch_total = tp_sum(switch_total).reshape(-1)
    logit_grad = switch_total * switch_value * (1.0 - switch_value)

    own_logit_grad = own_rows(logit_grad)[:, None]
    normed_two_grad = normed_two_grad + own_logit_grad * full_switch.astype(jnp.float32)[None, :]
    switch_gradient = jnp.sum(own_logit_grad * own_normed_two.astype(jnp.float32), axis=0)
    second_gain_gradient = jnp.sum(normed_two_grad * hidden * factor_two, axis=0)
    scaled_two = normed_two_grad * gain_two
    hidden_grad = (
        own_rows(grad_out)
        + factor_two * scaled_two
        - hidden * factor_two**3 * jnp.mean(scaled_two * hidden, axis=-1, keepdims=True)
    )
    own_attn_grad = low(hidden_grad)
    attn_grad_low = rows_gather(own_attn_grad)

    grad_down, grad_down_near = after((grad_down, grad_down_near), attn_grad_low)
    grad_down_parts = [grad_down[i * group : i * group + expert_hidden] for i in (0, 2)]
    grad_down_far = outer(
        low(grad_down_parts[1].astype(jnp.float32) + grad_down_near[1].astype(jnp.float32))
    )
    grad_down_terms = (grad_down_parts[0], grad_down_near[0], grad_down_far)
    shared_out_grad = after(shared_out_grad, own_attn_grad)
    shared_down_part = low(contract_rows(shared_out_grad, shared_inner))
    grad_shared_down = ring_scatter(shared_down_part).T.astype(jnp.float32)
    attn_grad_low = after(attn_grad_low, shared_down_part)
    attended_flat = low(times(attn_grad_low, full_output))
    attended_grad = by_head(attended_flat, heads_here)
    scores_again = masked_scores(queries, keys_rot, length_now, score_scale)
    probs_again = jnp.exp(scores_again - log_total)
    value_grad = jnp.einsum(
        "hts,htd->hsd", low(probs_again), attended_grad, preferred_element_type=jnp.float32
    )
    probs_grad = jnp.einsum(
        "htd,hsd->hts", attended_grad, values, preferred_element_type=jnp.float32
    )
    row_dot = jnp.sum(probs_again * probs_grad, axis=-1, keepdims=True)
    score_grad = low(probs_again * (probs_grad - row_dot))
    query_grad = (
        jnp.einsum("hts,hsd->htd", score_grad, keys_rot, preferred_element_type=jnp.float32)
        * score_scale
    )
    key_grad = (
        jnp.einsum("hts,htd->hsd", score_grad, queries, preferred_element_type=jnp.float32)
        * score_scale
    )
    query_pre_grad = low(side_by_side(rotate_backward(query_grad, cosine, sine)))
    key_pre_grad = low(side_by_side(rotate_backward(key_grad, cosine, sine)))
    value_pre_grad = low(side_by_side(value_grad))
    qkv_grad = jnp.concatenate([query_pre_grad, key_pre_grad, value_pre_grad], axis=1)
    bias_grad = jnp.sum(qkv_grad.astype(jnp.float32), axis=0)
    mixed = contract_rows(weighted, produced_home) + switch_value[:, None] * shared_part
    mixed = after(low(mixed), attended_flat)
    own_valid = own_rows(valid_float)
    output = rows_gather(from_ring(low(own_valid * (hidden + rows_scatter(mixed)[0])), 1))

    qkv_part = contract_rows(normed_one, qkv_grad)
    qkv_grad = after(qkv_grad, qkv_part)
    normed_one_grad, _ = rows_scatter(low(times_transpose(qkv_grad, full_qkv)))
    grad_in_terms, grad_down_terms = after((grad_in_terms, grad_down_terms), qkv_part)
    grad_expert_gate = from_ring(add_terms([t[:, :expert_hidden] for t in grad_in_terms]), 0)[None]
    grad_expert_up = from_ring(
        add_terms([t[:, group : group + expert_hidden] for t in grad_in_terms]), 0
    )[None]
    grad_expert_down = from_ring(add_terms(grad_down_terms), 1)[None]
    own_factor = own_rows(factor_one)
    first_gain_gradient = jnp.sum(normed_one_grad * own_inputs * own_factor, axis=0)
    scaled_one = normed_one_grad * gain_one
    token_gradient = (
        hidden_grad
        + own_factor * scaled_one
        - own_inputs * own_factor**3 * jnp.mean(scaled_one * own_inputs, axis=-1, keepdims=True)
    )
    own_token_gradient = from_ring(low(token_gradient), 1)
    token_gradient = rows_gather(own_token_gradient)
    grad_qkv = ring_scatter(
        jnp.concatenate(
            [low(qkv_part), low(contract_rows(attn_grad_low, attended_low))], axis=1
        ),
    ).astype(jnp.float32)
    grad_output_weight = grad_qkv[:, 3 * heads_width :].T
    grad_query_weight, grad_key_weight, grad_value_weight = (
        grad_qkv[:, i * heads_width : (i + 1) * heads_width] for i in range(3)
    )

    row_sums = tp_sum(jnp.stack([first_gain_gradient, second_gain_gradient, switch_gradient]))
    small_grad = jnp.concatenate(
        [
            from_ring(
                row_sums.reshape(3, ep_count, gain_part).transpose(1, 0, 2).reshape(ep_count, -1),
                0,
            ),
            bias_grad.reshape(3 * heads_here, ep_count, bias_part)
            .transpose(1, 0, 2)
            .reshape(ep_count, -1),
        ],
        axis=1,
    )
    small_grad = small_scatter(small_grad)
    first_gain_gradient, second_gain_gradient, switch_gradient = (
        small_grad[i * gain_part : (i + 1) * gain_part] for i in range(3)
    )
    bias_size = heads_here * bias_part
    grad_query_bias, grad_key_bias, grad_value_bias = (
        small_grad[3 * gain_part + i * bias_size : 3 * gain_part + (i + 1) * bias_size].reshape(
            heads_here, bias_part
        )
        for i in range(3)
    )
    return (
        output,
        token_gradient,
        first_gain_gradient,
        grad_query_weight,
        grad_key_weight,
        grad_value_weight,
        grad_query_bias,
        grad_key_bias,
        grad_value_bias,
        grad_output_weight,
        second_gain_gradient,
        grad_shared_gate,
        grad_shared_up,
        grad_shared_down,
        switch_gradient,
        grad_expert_gate,
        grad_expert_up,
        grad_expert_down,
    )


def solution(mesh):
    in_specs = (
        P("ep", None),
        P("ep"),
        P("ep", None),
        P("ep", None),
        P("ep", None),
        P("ep"),
        P("ep", "tp"),
        P("ep", "tp"),
        P("ep", "tp"),
        P("tp", "ep"),
        P("tp", "ep"),
        P("tp", "ep"),
        P("tp", "ep"),
        P("ep"),
        P("ep", "tp"),
        P("ep", "tp"),
        P("tp", "ep"),
        P("ep"),
        P("ep", None, "tp"),
        P("ep", None, "tp"),
        P("ep", "tp", None),
        P("ep", None),
    )
    out_specs = (
        P("ep", None),
        P("ep", None),
        P("ep"),
        P("ep", "tp"),
        P("ep", "tp"),
        P("ep", "tp"),
        P("tp", "ep"),
        P("tp", "ep"),
        P("tp", "ep"),
        P("tp", "ep"),
        P("ep"),
        P("ep", "tp"),
        P("ep", "tp"),
        P("tp", "ep"),
        P("ep"),
        P("ep", None, "tp"),
        P("ep", None, "tp"),
        P("ep", "tp", None),
    )

    return jax.shard_map(body, mesh=mesh, in_specs=in_specs, out_specs=out_specs, check_vma=False)
```
